512 devices in a mesh: depth: 8 (over x_lo, y), lat: 64 (over x_hi, z, core).
Axes of the slice: x: 4 (x_hi: 2, x_lo: 2; x = x_hi * 2 + x_lo), y: 4, z: 16, core: 2. Of those that a mesh axis runs over, the one named last changes fastest.
Arguments:
- source_field: bfloat16 [8, 2, 512, 2048], P(None, None, 'lat'), may hold values from -6 to 6
- receiver_field: bfloat16 [8, 2, 512, 2048], P(None, None, 'lat'), may hold values from -6 to 6
- freq_index: int32 [8], replicated, may hold values from 0 to 63
- slowness: float32 [8, 512, 2048], P('depth', 'lat'), may hold values from 0.5 to 2
- ffd_coef: float32 [8, 512, 2048], P('depth', 'lat'), may hold values from 0.04 to 0.12
- band: bfloat16 [16, 3, 128, 128], P('depth'), may hold values from -0.3125 to 0.3125
- image_mask: int32 [8, 512, 2048], P('depth', 'lat'), may hold values 0 or 1
Outputs:
- image: float32 [8, 512, 2048], P('depth', 'lat')
- gradient: float32 [8, 512, 2048], P('depth', 'lat')
The draws below stay inside these ranges and needn't reach their ends.
All inputs are finite; a program needn't handle non-finite values. No bound on the sum of `image_mask` on one device may be relied on, other than what follows from the above.
Results may differ from the reference program's by a relative error of at most 0.0035.
The reference program's roundings to bfloat16 on the way count: a program that leaves them out, or rounds other values in their place, can miss the bound.
Values may be sent and summed in bfloat16 or wider, within the bound.
No kernel may reach another device: no remote copies, remote signals or barrier semaphores. Data moves between devices by JAX's collectives and lax.ppermute only.
A program may use at most 64 MiB of HBM per device.

```python
import math
import jax
import jax.numpy as jnp
from jax import lax

LD = 1
NY = 2048
BLOCK = 128
HALO = 8
NFREQ = 64
NX = 512
NF = 8
L = 8
NBLK = 16


def touch_ends(values, stream_key, low, top_value):
    longest = values.shape.index(max(values.shape))
    spots = []
    for shift in (0, 1):
        where = [jax.random.randint(jax.random.fold_in(stream_key, axis), (), 0, length) for axis, length in enumerate(values.shape)]
        where[longest] = (where[longest] + shift) % values.shape[longest]
        spots.append(tuple(where))
    return values.at[spots[0]].set(low).at[spots[1]].set(top_value)


def steps_of(rng, dims, shards, low, largest):
    def one(position, parts):
        heights = jax.random.uniform(jax.random.fold_in(jax.random.fold_in(rng, 6), position), (parts,), jnp.float32, low / len(shards), largest / len(shards))
        return jnp.repeat(jnp.exp(heights), dims[position] // parts).reshape((-1,) + (1,) * (len(dims) - position - 1))

    gain = one(*shards[0])
    for cut in shards[1:]:
        gain = gain * one(*cut)
    return gain


def bell_draw(stream_key, shape, scale, limit, cuts=(), kind=jnp.bfloat16):
    entries = jax.random.normal(stream_key, shape, jnp.float32) * scale
    if len(cuts) > 0:
        entries = steps_of(stream_key, shape, cuts, -0.22, 0.18) * entries
    return jnp.clip(entries, min=-limit, max=limit).astype(kind)


def setup_inputs(seed: int = 0) -> dict:
    arg_keys = jax.random.split(jax.random.key(seed), 8)
    return {
        "source_field": bell_draw(arg_keys[0], (NF, 2, NX, NY), 1.0, 6.0, ((2, 64),)),
        "receiver_field": bell_draw(arg_keys[1], (NF, 2, NX, NY), 1.0, 6.0, ((2, 64),)),
        "freq_index": touch_ends(jax.random.randint(arg_keys[2], (NF,), 0, NFREQ), jax.random.fold_in(arg_keys[2], 1), 0, NFREQ - 1).astype(jnp.int32),
        "slowness": jnp.clip(jnp.exp(math.log(2.0) - 1.3862944 * jax.random.uniform(arg_keys[3], (L, NX, NY), jnp.float32) ** steps_of(arg_keys[3], (L, NX, NY), ((0, 8), (1, 64)), -0.2, 0.2)), 0.5, 2.0),
        "ffd_coef": jnp.clip(jnp.exp(math.log(0.12) - 1.0986123 * jax.random.uniform(arg_keys[4], (L, NX, NY), jnp.float32) ** steps_of(arg_keys[4], (L, NX, NY), ((0, 8), (1, 64)), -0.2, 0.2)), 0.04, 0.12),
        "band": bell_draw(arg_keys[5], (NBLK, 3, BLOCK, BLOCK), (3 * BLOCK) ** -0.5, 0.3125, ((0, 8),)),
        "image_mask": touch_ends((jax.random.randint(arg_keys[6], (L, NX, NY), 0, 4) < 3).astype(jnp.int32), jax.random.fold_in(arg_keys[6], 1), 0, 1),
    }


def roundtrip(values):
    return lax.optimization_barrier(values.astype(jnp.bfloat16)).astype(jnp.float32)


def stencil_full(field):
    rows = field.shape[-2]
    axis = field.ndim - 2
    widths = [(0, 0)] * field.ndim
    widths[axis] = (HALO, HALO)
    padded = jnp.pad(field, widths)
    total = jnp.zeros_like(field)
    for offset in range(1, HALO + 1):
        upper = lax.slice_in_dim(padded, HALO + offset, HALO + offset + rows, axis=axis)
        lower = lax.slice_in_dim(padded, HALO - offset, HALO - offset + rows, axis=axis)
        total = total + (0.25 / offset) * (upper + lower - 2.0 * field)
    return total


def band_full(field, band32):
    comps, rows, width = field.shape
    nblocks = band32.shape[0]
    block = band32.shape[2]
    tiles = field.reshape(comps, rows, nblocks, block)
    padded = jnp.pad(tiles, ((0, 0), (0, 0), (1, 1), (0, 0)))
    total = jnp.zeros(tiles.shape, jnp.float32)
    for offset in range(3):
        window = lax.slice_in_dim(padded, offset, offset + nblocks, axis=2)
        total = total + jnp.einsum("acjb,jbd->acjd", window, band32[:, offset], precision=lax.Precision.HIGHEST)
    return total.reshape(comps, rows, width)


def band_full_t(field, band32):
    comps, rows, width = field.shape
    nblocks = band32.shape[0]
    block = band32.shape[2]
    tiles = field.reshape(comps, rows, nblocks, block)
    total = jnp.zeros(tiles.shape, jnp.float32)
    for offset in range(3):
        moved = jnp.einsum("acjd,jbd->acjb", tiles, band32[:, offset], precision=lax.Precision.HIGHEST)
        padded = jnp.pad(moved, ((0, 0), (0, 0), (1, 1), (0, 0)))
        total = total + lax.slice_in_dim(padded, 2 - offset, 2 - offset + nblocks, axis=2)
    return total.reshape(comps, rows, width)


def level_step(field, omega, slow, coef, band32):
    theta = omega * slow
    cosine = jnp.cos(theta)
    sine_part = jnp.sin(theta)
    phased = jnp.stack([field[0] * cosine - field[1] * sine_part, field[0] * sine_part + field[1] * cosine])
    rounded = roundtrip(phased)
    lateral = band_full(rounded, band32) + stencil_full(rounded)
    return phased, jnp.stack([phased[0] - coef * lateral[1], phased[1] + coef * lateral[0]])


def adjoint_step(adjoint, phased, omega, slow, coef, band32):
    scaled = roundtrip(coef * adjoint)
    lateral = band_full_t(scaled, band32) + stencil_full(scaled)
    back_re = adjoint[0] + lateral[1]
    back_im = adjoint[1] - lateral[0]
    term = omega * (back_im * phased[0] - back_re * phased[1])
    theta = omega * slow
    cosine = jnp.cos(theta)
    sine_part = jnp.sin(theta)
    upward = jnp.stack([back_re * cosine + back_im * sine_part, back_im * cosine - back_re * sine_part])
    return term, upward


def reference(source_field, receiver_field, freq_index, slowness, ffd_coef, band, image_mask):
    levels = slowness.shape[0]
    count = freq_index.shape[0]
    omegas = 0.1 * (freq_index.astype(jnp.float32) + 1.0)
    level_ids = jnp.arange(levels, dtype=jnp.int32)
    band32 = band.astype(jnp.float32)

    def march(source, receiver, omega):
        def down(carry, inputs):
            field_s, field_q = carry
            slow, coef, level = inputs
            unused, new_s = level_step(field_s, omega, slow, coef, band32)
            phased_q, new_q = level_step(field_q, omega, slow, coef, band32)
            product = jnp.sum(new_s * new_q, axis=0)
            boundary = (level + 1) % LD == 0
            next_s = jnp.where(boundary, roundtrip(new_s), new_s)
            next_q = jnp.where(boundary, roundtrip(new_q), new_q)
            return (next_s, next_q), (product, new_s, phased_q)

        start = (source.astype(jnp.float32), receiver.astype(jnp.float32))
        final, outputs = lax.scan(down, start, (slowness, ffd_coef, level_ids))
        return outputs

    def image_part(total, inputs):
        products, states, phases = march(inputs[0], inputs[1], inputs[2])
        return total + products, None

    zero_levels = jnp.zeros(slowness.shape, jnp.float32)
    summed, unused = lax.scan(image_part, zero_levels, (source_field, receiver_field, omegas))
    image = summed / count
    masked = image_mask.astype(jnp.float32) * image

    def gradient_part(total, inputs):
        omega = inputs[2]
        products, states, phases = march(inputs[0], inputs[1], omega)

        def up(adjoint, items):
            slow, coef, weight, state, phased, level = items
            adjoint = adjoint + weight * state
            term, upward = adjoint_step(adjoint, phased, omega, slow, coef, band32)
            upward = jnp.where(level % LD == 0, roundtrip(upward), upward)
            return upward, term

        start = jnp.zeros(source_field.shape[1:], jnp.float32)
        final, terms = lax.scan(up, start, (slowness, ffd_coef, masked, states, phases, level_ids), reverse=True)
        return total + terms, None

    summed_grad, unused = lax.scan(gradient_part, zero_levels, (source_field, receiver_field, omegas))
    return image, summed_grad / count
```

```python
import functools
import jax
import jax.numpy as jnp
import numpy as np
from jax import lax
from jax.experimental import pallas as pl
from jax.experimental.pallas import tpu as pltpu
from jax.sharding import PartitionSpec as P

HALO = 8
BLOCK = 128
PAIR = 2 * BLOCK
CENTRE, EDGE, SLOW, COEF, PACKED = 0, 256, 384, 512, 640
VMEM = pl.BlockSpec(memory_space=pltpu.VMEM)
SMEM = pl.BlockSpec(memory_space=pltpu.SMEM)
F32, BF16 = jnp.float32, jnp.bfloat16


def stencil_weight(distance):
    if distance == 0:
        return sum(-0.5 / k for k in range(1, HALO + 1))
    return 0.25 / abs(distance) if abs(distance) <= HALO else 0.0


def stencil_matrix(combos, shift):
    small = np.zeros((HALO, HALO))
    for row in range(HALO):
        for source in range(HALO):
            small[row, source] = stencil_weight(shift + source - row)
    return np.kron(np.eye(combos), small)


def split_weights(matrix):
    high = matrix.astype(jnp.bfloat16)
    low = (matrix - high.astype(np.float64)).astype(jnp.bfloat16)
    return np.concatenate([high, low], axis=0)


def own_weights(combos):
    return split_weights(stencil_matrix(combos, 0))


def side_weights(combos):
    after, before = (stencil_matrix(combos, HALO), stencil_matrix(combos, -HALO))
    even = split_weights(np.concatenate([after, before], axis=1))
    odd = split_weights(np.concatenate([before, after], axis=1))
    return np.stack([even, odd])


def cos_sin(theta):
    turns = jnp.floor(theta * 0.6366197723675814 + 0.5)
    rest = theta - turns * 1.5703125
    rest = rest - turns * 4.837512969970703e-4
    rest = rest - turns * 7.549789948768648e-8
    square = rest * rest
    sine = rest + rest * square * (
        -1.6666654611e-1 + square * (8.3321608736e-3 + square * -1.9515295891e-4)
    )
    cosine = (
        1.0
        - 0.5 * square
        + square
        * square
        * (4.166664568298827e-2 + square * (-1.388731625493765e-3 + square * 2.443315711809948e-5))
    )
    quadrant = turns.astype(jnp.int32)
    swap = (quadrant & 1) == 1
    sine_out = jnp.where(swap, cosine, sine)
    cosine_out = jnp.where(swap, sine, cosine)
    sine_out = jnp.where((quadrant & 2) == 2, -sine_out, sine_out)
    cosine_out = jnp.where(((quadrant + 1) & 2) == 2, -cosine_out, cosine_out)
    return (cosine_out, sine_out)


def dot(left, right):
    return jnp.dot(left, right, preferred_element_type=F32)


def dot_t(left, right):
    return lax.dot_general(left, right, (((1,), (1,)), ((), ())), preferred_element_type=F32)


def columns(chunk):
    return slice(chunk * PAIR, (chunk + 1) * PAIR)


def joined(packed_ref, level, base, chunk):
    start = base + chunk * 2 * HALO
    both = packed_ref[level, start : start + 2 * HALO, :].astype(F32)
    return both[:HALO] + both[HALO:]


def pack_kernel(slow_ref, coef_ref, band_ref, out_ref):
    copies = out_ref.shape[0]

    def write(rows, cols, value):
        for copy in range(copies):
            out_ref[copy, rows, cols] = value

    left, right = (slice(0, BLOCK), slice(BLOCK, PAIR))
    write(slice(0, BLOCK), left, band_ref[0, 1])
    write(slice(0, BLOCK), right, band_ref[1, 0])
    write(slice(BLOCK, PAIR), left, band_ref[0, 2])
    write(slice(BLOCK, PAIR), right, band_ref[1, 1])
    write(slice(EDGE, EDGE + BLOCK), left, band_ref[0, 0])
    write(slice(EDGE, EDGE + BLOCK), right, band_ref[1, 2])
    for ref, base in ((slow_ref, SLOW), (coef_ref, COEF)):
        for chunk in range(ref.shape[2] // PAIR):
            value = ref[0, :, columns(chunk)]
            high = value.astype(BF16).astype(F32)
            pair = jnp.concatenate([high, value - high], axis=0).astype(BF16)
            start = base + chunk * 2 * HALO
            write(slice(start, start + 2 * HALO), slice(0, PAIR), pair)


def phase(fields, cosine, sine):
    parts = []
    for member in range(fields.shape[0] // (2 * HALO)):
        base = member * 2 * HALO
        real, imag = (fields[base : base + HALO], fields[base + HALO : base + 2 * HALO])
        parts.append(real * cosine - imag * sine)
        parts.append(real * sine + imag * cosine)
    return jnp.concatenate(parts, axis=0)


def first_kernel(omega_ref, packed_ref, fields_ref, rows_ref, phased_ref, angle_ref):
    omega = omega_ref[0]
    for chunk in range(packed_ref.shape[0]):
        cols = columns(chunk)
        cosine, sine = cos_sin(omega * joined(packed_ref, 0, SLOW, chunk))
        angle_ref[0:HALO, cols] = cosine
        angle_ref[HALO : 2 * HALO, cols] = sine
        phased = phase(fields_ref[:, cols].astype(F32), cosine, sine)
        phased_ref[:, cols] = phased
        rows_ref[:, cols] = phased.astype(BF16)


def middle_kernel(level, omega_ref, packed_ref, weights_ref, rows_ref, lateral_ref, *angle_refs):
    omega = omega_ref[0]
    pairs = packed_ref.shape[0]
    height = rows_ref.shape[0]
    for pair in range(pairs):
        cols = columns(pair)
        rows = rows_ref[:, cols]
        total = dot(rows, packed_ref[pair, CENTRE : CENTRE + PAIR, :])
        spread = dot(weights_ref[...], rows)
        total = total + (spread[:height] + spread[height:])
        zero = jnp.zeros((height, BLOCK), F32)
        left, right = (zero, zero)
        if pair > 0:
            before = rows_ref[:, pair * PAIR - BLOCK : pair * PAIR]
            left = dot(before, packed_ref[pair, EDGE : EDGE + BLOCK, 0:BLOCK])
        if pair < pairs - 1:
            after = rows_ref[:, (pair + 1) * PAIR : (pair + 1) * PAIR + BLOCK]
            right = dot(after, packed_ref[pair, EDGE : EDGE + BLOCK, BLOCK:PAIR])
        lateral_ref[:, cols] = total + jnp.concatenate([left, right], axis=1)
        if angle_refs:
            cosine, sine = cos_sin(omega * joined(packed_ref, level + 1, SLOW, pair))
            angle_refs[0][0:HALO, cols] = cosine
            angle_refs[0][HALO : 2 * HALO, cols] = sine


def sides(weights_ref, first_ref, second_ref, cols):
    both = jnp.concatenate([first_ref[:, cols], second_ref[:, cols]], axis=0)
    spread = dot(weights_ref[...], both)
    height = first_ref.shape[0]
    return spread[:height] + spread[height:]


def step_kernel(level, last, *refs):
    if last:
        packed, weights, lateral, first, second, phased, state, product = refs
    else:
        packed, weights, lateral, first, second, phased, angle = refs[:7]
        state, product, rows_next, phased_next = refs[7:]
    for chunk in range(packed.shape[0]):
        cols = columns(chunk)
        total = lateral[:, cols] + sides(weights, first, second, cols)
        coef = joined(packed, level, COEF, chunk)
        value = phased[:, cols]
        part = [slice(k * HALO, (k + 1) * HALO) for k in range(4)]
        source_re = value[part[0]] - coef * total[part[1]]
        source_im = value[part[1]] + coef * total[part[0]]
        receiver_re = value[part[2]] - coef * total[part[3]]
        receiver_im = value[part[3]] + coef * total[part[2]]
        state[0:HALO, cols] = source_re
        state[HALO : 2 * HALO, cols] = source_im
        product[:, cols] = source_re * receiver_re + source_im * receiver_im
        if not last:
            stepped = jnp.concatenate([source_re, source_im, receiver_re, receiver_im], axis=0)
            entering = stepped.astype(BF16).astype(F32)
            cosine, sine = (angle[0:HALO, cols], angle[HALO : 2 * HALO, cols])
            following = phase(entering, cosine, sine)
            phased_next[:, cols] = following
            rows_next[:, cols] = following.astype(BF16)


def image_kernel(parts_ref, mask_ref, image_ref, masked_ref):
    count = parts_ref.shape[0]
    total = parts_ref[0]
    for member in range(1, count):
        total = total + parts_ref[member]
    image = total / count
    image_ref[0] = image
    masked = mask_ref[0].astype(F32) * image
    for copy in range(count):
        masked_ref[copy] = masked


def gradient_kernel(parts_ref, gradient_ref):
    count = parts_ref.shape[0]
    total = parts_ref[0]
    for member in range(1, count):
        total = total + parts_ref[member]
    gradient_ref[0] = total / count


def scaled_rows(adjoint, coef):
    return jnp.concatenate([adjoint[:HALO] * coef, adjoint[HALO:] * coef], axis=0).astype(BF16)


def weighted(masked, state):
    return jnp.concatenate([masked * state[:HALO], masked * state[HALO:]], axis=0)


def adjoint_kernel(level, packed, masked, state, adjoint, scaled):
    for chunk in range(packed.shape[0]):
        cols = columns(chunk)
        value = weighted(masked[level, :, cols], state[:, cols])
        adjoint[:, cols] = value
        scaled[:, cols] = scaled_rows(value, joined(packed, level, COEF, chunk))


def middle_back_kernel(packed_ref, weights_ref, rows_ref, lateral_ref):
    pairs = packed_ref.shape[0]
    height = rows_ref.shape[0]
    for pair in range(pairs):
        cols = columns(pair)
        rows = rows_ref[:, cols]
        total = dot_t(rows, packed_ref[pair, CENTRE : CENTRE + PAIR, :])
        spread = dot(weights_ref[...], rows)
        total = total + (spread[:height] + spread[height:])
        zero = jnp.zeros((height, BLOCK), F32)
        left, right = (zero, zero)
        if pair > 0:
            before = rows_ref[:, pair * PAIR - BLOCK : pair * PAIR]
            left = dot_t(before, packed_ref[pair - 1, EDGE : EDGE + BLOCK, BLOCK:PAIR])
        if pair < pairs - 1:
            after = rows_ref[:, (pair + 1) * PAIR : (pair + 1) * PAIR + BLOCK]
            right = dot_t(after, packed_ref[pair + 1, EDGE : EDGE + BLOCK, 0:BLOCK])
        lateral_ref[:, cols] = total + jnp.concatenate([left, right], axis=1)


def back_kernel(level, last, *refs):
    if last:
        omega, packed, weights, lateral, first, second, adjoint, phased, term = refs
    else:
        omega, packed, weights, lateral, first, second, adjoint, phased = refs[:8]
        angle, masked, state, term, adjoint_next, scaled_next = refs[8:]
    for chunk in range(packed.shape[0]):
        cols = columns(chunk)
        total = lateral[:, cols] + sides(weights, first, second, cols)
        value = adjoint[:, cols]
        back_re = value[:HALO] + total[HALO:]
        back_im = value[HALO:] - total[:HALO]
        phase_re = phased[2 * HALO : 3 * HALO, cols]
        phase_im = phased[3 * HALO : 4 * HALO, cols]
        term[:, cols] = omega[0] * (back_im * phase_re - back_re * phase_im)
        if not last:
            cosine, sine = (angle[0:HALO, cols], angle[HALO : 2 * HALO, cols])
            upward = jnp.concatenate(
                [back_re * cosine + back_im * sine, back_im * cosine - back_re * sine], axis=0
            )
            upward = upward.astype(BF16).astype(F32)
            following = weighted(masked[level - 1, :, cols], state[:, cols]) + upward
            adjoint_next[:, cols] = following
            scaled_next[:, cols] = scaled_rows(following, joined(packed, level - 1, COEF, chunk))


def call(kernel, name, outs, cost, *args):
    shapes = [jax.ShapeDtypeStruct(shape, kind) for shape, kind in outs]
    return pl.pallas_call(
        kernel,
        name=name,
        out_shape=shapes,
        in_specs=[SMEM if arg.shape == (1,) else VMEM for arg in args],
        out_specs=[VMEM] * len(shapes),
        cost_estimate=pl.CostEstimate(flops=cost, bytes_accessed=1 << 20, transcendentals=0),
    )(*args)


def swapped(rows):
    size = lax.axis_size("lat")
    received = []
    for offset in (0, 1):
        pairs = [(i, i + 1) for i in range(offset, size - 1, 2)]
        route = [(a, b) for a, b in pairs] + [(b, a) for a, b in pairs]
        received.append(lax.ppermute(rows, "lat", route))
    return received


def exchanged(parts):
    return lax.all_to_all(parts, "depth", 0, 0)


def per_device(source_field, receiver_field, freq_index, slowness, ffd_coef, band, image_mask):
    sections = lax.axis_size("depth")
    member = lax.axis_index("depth")
    height, width = slowness.shape[1:]
    levels = sections
    omega = 0.1 * (lax.dynamic_slice_in_dim(freq_index, member, 1).astype(F32) + 1.0)
    odd = lax.rem(lax.axis_index("lat"), 2)
    side_fore = jnp.where(odd == 1, *side_weights(4)[::-1])
    side_back = jnp.where(odd == 1, *side_weights(2)[::-1])
    own_fore, own_back = (jnp.asarray(own_weights(4)), jnp.asarray(own_weights(2)))
    source = lax.dynamic_index_in_dim(source_field, member, 0, keepdims=False)
    receiver = lax.dynamic_index_in_dim(receiver_field, member, 0, keepdims=False)
    fields = jnp.concatenate([source, receiver]).reshape(4 * height, width)

    wide, half, single = ((4 * height, width), (2 * height, width), (height, width))
    (packed,) = call(
        pack_kernel, "pack", [((sections, PACKED, PAIR), BF16)], 1000, slowness, ffd_coef, band
    )
    packed = exchanged(packed)
    rows, phased, angle = call(
        first_kernel, "first", [(wide, BF16), (wide, F32), (half, F32)], 1000, omega, packed, fields
    )
    states, products, phases, angles = ([], [], [phased], [angle])
    for level in range(levels):
        last = level == levels - 1
        first, second = swapped(rows)
        outs = [(wide, F32)] + ([] if last else [(half, F32)])
        lateral, *more = call(
            functools.partial(middle_kernel, level),
            "middle",
            outs,
            1 << 28,
            omega,
            packed,
            own_fore,
            rows,
        )
        angles += more
        outs = [(half, F32), (single, F32)] + ([] if last else [(wide, BF16), (wide, F32)])
        args = [packed, side_fore, lateral, first, second, phased] + more
        state, product, *more = call(
            functools.partial(step_kernel, level, last), "step", outs, 1 << 20, *args
        )
        states.append(state)
        products.append(product)
        if not last:
            rows, phased = more
            phases.append(phased)

    image, masked = call(
        image_kernel,
        "image",
        [((1,) + single, F32), ((sections,) + single, F32)],
        1000,
        exchanged(jnp.stack(products)),
        image_mask,
    )
    masked = exchanged(masked)

    level = levels - 1
    adjoint, scaled = call(
        functools.partial(adjoint_kernel, level),
        "adjoint",
        [(half, F32), (half, BF16)],
        1000,
        packed,
        masked,
        states[level],
    )
    terms = [None] * levels
    for level in reversed(range(levels)):
        last = level == 0
        first, second = swapped(scaled)
        (lateral,) = call(
            middle_back_kernel, "middle_back", [(half, F32)], 1 << 28, packed, own_back, scaled
        )
        args = [omega, packed, side_back, lateral, first, second, adjoint, phases[level]]
        outs = [(single, F32)]
        if not last:
            args += [angles[level], masked, states[level - 1]]
            outs += [(half, F32), (half, BF16)]
        terms[level], *more = call(
            functools.partial(back_kernel, level, last), "back", outs, 1 << 20, *args
        )
        if not last:
            adjoint, scaled = more
    (gradient,) = call(
        gradient_kernel, "gradient", [((1,) + single, F32)], 1000, exchanged(jnp.stack(terms))
    )
    return (image, gradient)


def solution(mesh):
    return jax.shard_map(
        per_device,
        mesh=mesh,
        in_specs=(
            P(None, None, "lat", None),
            P(None, None, "lat", None),
            P(),
            P("depth", "lat", None),
            P("depth", "lat", None),
            P("depth", None, None, None),
            P("depth", "lat", None),
        ),
        out_specs=(P("depth", "lat", None), P("depth", "lat", None)),
        check_vma=False,
    )
```

```python
import functools
import jax
import jax.numpy as jnp
import numpy as np
from jax import lax
from jax.experimental import pallas as pl
from jax.experimental.pallas import tpu as pltpu
from jax.sharding import PartitionSpec as P

HALO = 8
BLOCK = 128
PAIR = 2 * BLOCK
CENTRE, EDGE, SLOW, COEF, PACKED = 0, 256, 384, 640, 704
VMEM = pl.BlockSpec(memory_space=pltpu.VMEM)
SMEM = pl.BlockSpec(memory_space=pltpu.SMEM)
F32, BF16 = jnp.float32, jnp.bfloat16


def stencil_weight(distance):
    if distance == 0:
        return sum(-0.5 / k for k in range(1, HALO + 1))
    return 0.25 / abs(distance) if abs(distance) <= HALO else 0.0


def stencil_matrix(combos, shift):
    small = np.zeros((HALO, HALO))
    for row in range(HALO):
        for source in range(HALO):
            small[row, source] = stencil_weight(shift + source - row)
    return np.kron(np.eye(combos), small)


def split_weights(matrix):
    high = matrix.astype(jnp.bfloat16)
    low = (matrix - high.astype(np.float64)).astype(jnp.bfloat16)
    return np.concatenate([high, low], axis=0)


def own_weights(combos):
    return split_weights(stencil_matrix(combos, 0))


def side_weights(combos):
    after, before = (stencil_matrix(combos, HALO), stencil_matrix(combos, -HALO))
    even = split_weights(np.concatenate([before, after], axis=1))
    odd = split_weights(np.concatenate([after, before], axis=1))
    return np.stack([even, odd])


def cos_sin(theta):
    turns = jnp.floor(theta * 0.6366197723675814 + 0.5)
    rest = theta - turns * 1.5703125
    rest = rest - turns * 4.837512969970703e-4
    rest = rest - turns * 7.549789948768648e-8
    square = rest * rest
    sine = rest + rest * square * (
        -1.6666654611e-1 + square * (8.3321608736e-3 + square * -1.9515295891e-4)
    )
    cosine = (
        1.0
        - 0.5 * square
        + square
        * square
        * (4.166664568298827e-2 + square * (-1.388731625493765e-3 + square * 2.443315711809948e-5))
    )
    quadrant = turns.astype(jnp.int32)
    swap = (quadrant & 1) == 1
    sine_out = jnp.where(swap, cosine, sine)
    cosine_out = jnp.where(swap, sine, cosine)
    sine_out = jnp.where((quadrant & 2) == 2, -sine_out, sine_out)
    cosine_out = jnp.where(((quadrant + 1) & 2) == 2, -cosine_out, cosine_out)
    return (cosine_out, sine_out)


def dot(left, right):
    return jnp.dot(left, right, preferred_element_type=F32)


def dot_t(left, right):
    return lax.dot_general(left, right, (((1,), (1,)), ((), ())), preferred_element_type=F32)


def columns(chunk):
    return slice(chunk * PAIR, (chunk + 1) * PAIR)


def slowness_of(packed_ref, level, chunk):
    start = SLOW + chunk * 4 * HALO
    value = packed_ref[level, start : start + 4 * HALO, :].astype(F32)
    return value[:HALO] + value[HALO : 2 * HALO] + value[2 * HALO : 3 * HALO]


def coef_of(packed_ref, level, chunk):
    start = SLOW + chunk * 4 * HALO + 2 * HALO
    high = packed_ref[level, start : start + 2 * HALO, :].astype(F32)[HALO:]
    start = COEF + chunk // 2 * 2 * HALO
    low = packed_ref[level, start : start + 2 * HALO, :].astype(F32)
    return high + (low[:HALO] if chunk % 2 == 0 else low[HALO:])


def rounded(value):
    return value.astype(BF16).astype(F32)


def pack_kernel(slow_ref, coef_ref, band_ref, out_ref):
    copies = out_ref.shape[0]

    def write(rows, cols, value):
        for copy in range(copies):
            out_ref[copy, rows, cols] = value

    left, right = (slice(0, BLOCK), slice(BLOCK, PAIR))
    write(slice(0, BLOCK), left, band_ref[0, 1])
    write(slice(0, BLOCK), right, band_ref[1, 0])
    write(slice(BLOCK, PAIR), left, band_ref[0, 2])
    write(slice(BLOCK, PAIR), right, band_ref[1, 1])
    write(slice(EDGE, EDGE + BLOCK), left, band_ref[0, 0])
    write(slice(EDGE, EDGE + BLOCK), right, band_ref[1, 2])
    lows = []
    for chunk in range(slow_ref.shape[2] // PAIR):
        slow = slow_ref[0, :, columns(chunk)]
        coef = coef_ref[0, :, columns(chunk)]
        high = rounded(slow)
        middle = rounded(slow - high)
        coef_high = rounded(coef)
        lows.append(coef - coef_high)
        pieces = jnp.concatenate([high, middle, slow - high - middle, coef_high], axis=0)
        start = SLOW + chunk * 4 * HALO
        write(slice(start, start + 4 * HALO), slice(0, PAIR), pieces.astype(BF16))
    for half in range(len(lows) // 2):
        start = COEF + half * 2 * HALO
        pieces = jnp.concatenate(lows[2 * half : 2 * half + 2], axis=0)
        write(slice(start, start + 2 * HALO), slice(0, PAIR), pieces.astype(BF16))


def phase(fields, cosine, sine):
    parts = []
    for member in range(fields.shape[0] // (2 * HALO)):
        base = member * 2 * HALO
        real, imag = (fields[base : base + HALO], fields[base + HALO : base + 2 * HALO])
        parts.append(real * cosine - imag * sine)
        parts.append(real * sine + imag * cosine)
    return jnp.concatenate(parts, axis=0)


def first_kernel(omega_ref, packed_ref, fields_ref, rows_ref, phased_ref, angle_ref):
    omega = omega_ref[0]
    for chunk in range(packed_ref.shape[0]):
        cols = columns(chunk)
        cosine, sine = cos_sin(omega * slowness_of(packed_ref, 0, chunk))
        angle_ref[0:HALO, cols] = cosine
        angle_ref[HALO : 2 * HALO, cols] = sine
        phased = phase(fields_ref[:, cols].astype(F32), cosine, sine)
        phased_ref[:, cols] = phased
        rows_ref[:, cols] = phased.astype(BF16)


def middle_kernel(level, omega_ref, packed_ref, weights_ref, rows_ref, lateral_ref, *angle_refs):
    omega = omega_ref[0]
    pairs = packed_ref.shape[0]
    height = rows_ref.shape[0]
    for pair in range(pairs):
        cols = columns(pair)
        rows = rows_ref[:, cols]
        total = dot(rows, packed_ref[pair, CENTRE : CENTRE + PAIR, :])
        spread = dot(weights_ref[...], rows)
        total = total + (spread[:height] + spread[height:])
        zero = jnp.zeros((height, BLOCK), F32)
        left, right = (zero, zero)
        if pair > 0:
            before = rows_ref[:, pair * PAIR - BLOCK : pair * PAIR]
            left = dot(before, packed_ref[pair, EDGE : EDGE + BLOCK, 0:BLOCK])
        if pair < pairs - 1:
            after = rows_ref[:, (pair + 1) * PAIR : (pair + 1) * PAIR + BLOCK]
            right = dot(after, packed_ref[pair, EDGE : EDGE + BLOCK, BLOCK:PAIR])
        lateral_ref[:, cols] = total + jnp.concatenate([left, right], axis=1)
        if angle_refs:
            cosine, sine = cos_sin(omega * slowness_of(packed_ref, level + 1, pair))
            angle_refs[0][0:HALO, cols] = cosine
            angle_refs[0][HALO : 2 * HALO, cols] = sine


def sides(weights_ref, first_ref, second_ref, cols):
    both = jnp.concatenate([first_ref[:, cols], second_ref[:, cols]], axis=0)
    spread = dot(weights_ref[...], both)
    height = first_ref.shape[0]
    return spread[:height] + spread[height:]


def step_kernel(level, last, *refs):
    if last:
        packed, weights, lateral, first, second, phased, state, product = refs
    else:
        packed, weights, lateral, first, second, phased, angle = refs[:7]
        state, product, rows_next, phased_next = refs[7:]
    for chunk in range(packed.shape[0]):
        cols = columns(chunk)
        total = lateral[:, cols] + sides(weights, first, second, cols)
        coef = coef_of(packed, level, chunk)
        value = phased[:, cols]
        part = [slice(k * HALO, (k + 1) * HALO) for k in range(4)]
        source_re = value[part[0]] - coef * total[part[1]]
        source_im = value[part[1]] + coef * total[part[0]]
        receiver_re = value[part[2]] - coef * total[part[3]]
        receiver_im = value[part[3]] + coef * total[part[2]]
        state[0:HALO, cols] = source_re
        state[HALO : 2 * HALO, cols] = source_im
        product[:, cols] = source_re * receiver_re + source_im * receiver_im
        if not last:
            stepped = jnp.concatenate([source_re, source_im, receiver_re, receiver_im], axis=0)
            entering = stepped.astype(BF16).astype(F32)
            cosine, sine = (angle[0:HALO, cols], angle[HALO : 2 * HALO, cols])
            following = phase(entering, cosine, sine)
            phased_next[:, cols] = following
            rows_next[:, cols] = following.astype(BF16)


def image_kernel(parts_ref, mask_ref, image_ref, masked_ref):
    count = parts_ref.shape[0]
    total = parts_ref[0]
    for member in range(1, count):
        total = total + parts_ref[member]
    image = total / count
    image_ref[0] = image
    masked = mask_ref[0].astype(F32) * image
    for copy in range(count):
        masked_ref[copy] = masked


def gradient_kernel(parts_ref, gradient_ref):
    count = parts_ref.shape[0]
    total = parts_ref[0]
    for member in range(1, count):
        total = total + parts_ref[member]
    gradient_ref[0] = total / count


def scaled_rows(adjoint, coef):
    return jnp.concatenate([adjoint[:HALO] * coef, adjoint[HALO:] * coef], axis=0).astype(BF16)


def weighted(masked, state):
    return jnp.concatenate([masked * state[:HALO], masked * state[HALO:]], axis=0)


def adjoint_kernel(level, packed, masked, state, adjoint, scaled):
    for chunk in range(packed.shape[0]):
        cols = columns(chunk)
        value = weighted(masked[level, :, cols], state[:, cols])
        adjoint[:, cols] = value
        scaled[:, cols] = scaled_rows(value, coef_of(packed, level, chunk))


def middle_back_kernel(packed_ref, weights_ref, rows_ref, lateral_ref):
    pairs = packed_ref.shape[0]
    height = rows_ref.shape[0]
    for pair in range(pairs):
        cols = columns(pair)
        rows = rows_ref[:, cols]
        total = dot_t(rows, packed_ref[pair, CENTRE : CENTRE + PAIR, :])
        spread = dot(weights_ref[...], rows)
        total = total + (spread[:height] + spread[height:])
        zero = jnp.zeros((height, BLOCK), F32)
        left, right = (zero, zero)
        if pair > 0:
            before = rows_ref[:, pair * PAIR - BLOCK : pair * PAIR]
            left = dot_t(before, packed_ref[pair - 1, EDGE : EDGE + BLOCK, BLOCK:PAIR])
        if pair < pairs - 1:
            after = rows_ref[:, (pair + 1) * PAIR : (pair + 1) * PAIR + BLOCK]
            right = dot_t(after, packed_ref[pair + 1, EDGE : EDGE + BLOCK, 0:BLOCK])
        lateral_ref[:, cols] = total + jnp.concatenate([left, right], axis=1)


def back_kernel(level, last, *refs):
    if last:
        omega, packed, weights, lateral, first, second, adjoint, phased, term = refs
    else:
        omega, packed, weights, lateral, first, second, adjoint, phased = refs[:8]
        angle, masked, state, term, adjoint_next, scaled_next = refs[8:]
    for chunk in range(packed.shape[0]):
        cols = columns(chunk)
        total = lateral[:, cols] + sides(weights, first, second, cols)
        value = adjoint[:, cols]
        back_re = value[:HALO] + total[HALO:]
        back_im = value[HALO:] - total[:HALO]
        phase_re = phased[2 * HALO : 3 * HALO, cols]
        phase_im = phased[3 * HALO : 4 * HALO, cols]
        term[:, cols] = omega[0] * (back_im * phase_re - back_re * phase_im)
        if not last:
            cosine, sine = (angle[0:HALO, cols], angle[HALO : 2 * HALO, cols])
            upward = jnp.concatenate(
                [back_re * cosine + back_im * sine, back_im * cosine - back_re * sine], axis=0
            )
            upward = upward.astype(BF16).astype(F32)
            following = weighted(masked[level - 1, :, cols], state[:, cols]) + upward
            adjoint_next[:, cols] = following
            scaled_next[:, cols] = scaled_rows(following, coef_of(packed, level - 1, chunk))


def call(kernel, name, outs, cost, *args, local=True):
    kind_of = pltpu.VMEM if local else jax.ShapeDtypeStruct
    placed = []
    for arg in args:
        scalar = arg.shape == (1,)
        placed.append(arg if scalar else pltpu.with_memory_space_constraint(arg, pltpu.VMEM))
    return pl.pallas_call(
        kernel,
        name=name,
        out_shape=[kind_of(shape, kind) for shape, kind in outs],
        in_specs=[SMEM if arg.shape == (1,) else VMEM for arg in args],
        out_specs=[VMEM] * len(outs),
        cost_estimate=pl.CostEstimate(flops=cost, bytes_accessed=1 << 20, transcendentals=0),
        compiler_params=pltpu.CompilerParams(vmem_limit_bytes=8 << 20),
    )(*placed)


def stack_kernel(*refs):
    for index, ref in enumerate(refs[:-1]):
        refs[-1][index] = ref[...]


def stacked(parts):
    shape = (len(parts),) + parts[0].shape
    return call(stack_kernel, "stack", [(shape, F32)], 1000, *parts)[0]


def frequency_of(depth, lat, sections, size):
    upper = lat >= size // 2
    return (depth + upper * (sections // 2)) % sections


def swapped(rows):
    sections, size = (lax.axis_size("depth"), lax.axis_size("lat"))
    place = {}
    for depth in range(sections):
        for lat in range(size):
            place[frequency_of(depth, lat, sections, size), lat] = depth * size + lat
    received = []
    for offset in (1, 0):
        route = []
        for member in range(sections):
            for lat in range(offset, size - 1, 2):
                one, other = (place[member, lat], place[member, lat + 1])
                route += [(one, other), (other, one)]
        received.append(lax.ppermute(rows, ("depth", "lat"), route))
    return received


def exchanged(parts):
    return lax.all_to_all(parts, "depth", 0, 0)


def per_device(source_field, receiver_field, freq_index, slowness, ffd_coef, band, image_mask):
    sections = lax.axis_size("depth")
    lat, size = (lax.axis_index("lat"), lax.axis_size("lat"))
    member = frequency_of(lax.axis_index("depth"), lat, sections, size)
    height, width = slowness.shape[1:]
    levels = sections
    omega = 0.1 * (lax.dynamic_slice_in_dim(freq_index, member, 1).astype(F32) + 1.0)
    odd = lax.rem(lat, 2)
    side_fore = jnp.where(odd == 1, *side_weights(4)[::-1])
    side_back = jnp.where(odd == 1, *side_weights(2)[::-1])
    own_fore, own_back = (jnp.asarray(own_weights(4)), jnp.asarray(own_weights(2)))
    source = lax.dynamic_index_in_dim(source_field, member, 0, keepdims=False)
    receiver = lax.dynamic_index_in_dim(receiver_field, member, 0, keepdims=False)
    fields = jnp.concatenate([source, receiver]).reshape(4 * height, width)

    wide, half, single = ((4 * height, width), (2 * height, width), (height, width))
    (packed,) = call(
        pack_kernel, "pack", [((sections, PACKED, PAIR), BF16)], 1000, slowness, ffd_coef, band
    )
    packed = exchanged(packed)
    rows, phased, angle = call(
        first_kernel, "first", [(wide, BF16), (wide, F32), (half, F32)], 1000, omega, packed, fields
    )
    states, products, phases, angles = ([], [], [phased], [angle])
    for level in range(levels):
        last = level == levels - 1
        first, second = swapped(rows)
        outs = [(wide, F32)] + ([] if last else [(half, F32)])
        lateral, *more = call(
            functools.partial(middle_kernel, level),
            "middle",
            outs,
            1 << 28,
            omega,
            packed,
            own_fore,
            rows,
        )
        angles += more
        outs = [(half, F32), (single, F32)] + ([] if last else [(wide, BF16), (wide, F32)])
        args = [packed, side_fore, lateral, first, second, phased] + more
        state, product, *more = call(
            functools.partial(step_kernel, level, last), "step", outs, 1 << 20, *args
        )
        states.append(state)
        products.append(product)
        if not last:
            rows, phased = more
            phases.append(phased)

    image, masked = call(
        image_kernel,
        "image",
        [((1,) + single, F32), ((sections,) + single, F32)],
        1000,
        exchanged(stacked(products)),
        image_mask,
    )
    masked = exchanged(masked)

    level = levels - 1
    adjoint, scaled = call(
        functools.partial(adjoint_kernel, level),
        "adjoint",
        [(half, F32), (half, BF16)],
        1000,
        packed,
        masked,
        states[level],
    )
    terms = [None] * levels
    for level in reversed(range(levels)):
        last = level == 0
        first, second = swapped(scaled)
        (lateral,) = call(
            middle_back_kernel, "middle_back", [(half, F32)], 1 << 28, packed, own_back, scaled
        )
        args = [omega, packed, side_back, lateral, first, second, adjoint, phases[level]]
        outs = [(single, F32)]
        if not last:
            args += [angles[level], masked, states[level - 1]]
            outs += [(half, F32), (half, BF16)]
        terms[level], *more = call(
            functools.partial(back_kernel, level, last), "back", outs, 1 << 20, *args
        )
        if not last:
            adjoint, scaled = more
    (gradient,) = call(
        gradient_kernel, "gradient", [((1,) + single, F32)], 1000, exchanged(stacked(terms)),
        local=False,
    )
    return (image, gradient)


def solution(mesh):
    return jax.shard_map(
        per_device,
        mesh=mesh,
        in_specs=(
            P(None, None, "lat", None),
            P(None, None, "lat", None),
            P(),
            P("depth", "lat", None),
            P("depth", "lat", None),
            P("depth", None, None, None),
            P("depth", "lat", None),
        ),
        out_specs=(P("depth", "lat", None), P("depth", "lat", None)),
        check_vma=False,
    )
```

```python
import functools
import jax
import jax.numpy as jnp
import numpy as np
from jax import lax
from jax.experimental import pallas as pl
from jax.experimental.pallas import tpu as pltpu
from jax.sharding import PartitionSpec as P

HALO = 8
BLOCK = 128
PAIR = 2 * BLOCK
PIECE = BLOCK + BLOCK // 2
VMEM = pl.BlockSpec(memory_space=pltpu.VMEM)
SMEM = pl.BlockSpec(memory_space=pltpu.SMEM)
F32, BF16 = jnp.float32, jnp.bfloat16


def stencil_weight(distance):
    if distance == 0:
        return sum(-0.5 / k for k in range(1, HALO + 1))
    return 0.25 / abs(distance) if abs(distance) <= HALO else 0.0


def stencil_matrix(combos, shift):
    small = np.zeros((HALO, HALO))
    for row in range(HALO):
        for source in range(HALO):
            small[row, source] = stencil_weight(shift + source - row)
    return np.kron(np.eye(combos), small)


def split_weights(matrix):
    high = matrix.astype(jnp.bfloat16)
    low = (matrix - high.astype(np.float64)).astype(jnp.bfloat16)
    return np.concatenate([high, low], axis=0)


def own_weights(combos):
    return split_weights(stencil_matrix(combos, 0))


def side_weights(combos):
    after, before = (stencil_matrix(combos, HALO), stencil_matrix(combos, -HALO))
    even = split_weights(np.concatenate([before, after], axis=1))
    odd = split_weights(np.concatenate([after, before], axis=1))
    return np.stack([even, odd])


def cos_sin(theta):
    turns = jnp.floor(theta * 0.6366197723675814 + 0.5)
    rest = theta - turns * 1.5703125
    rest = rest - turns * 4.837512969970703e-4
    rest = rest - turns * 7.549789948768648e-8
    square = rest * rest
    sine = rest + rest * square * (
        -1.6666654611e-1 + square * (8.3321608736e-3 + square * -1.9515295891e-4)
    )
    cosine = (
        1.0
        - 0.5 * square
        + square
        * square
        * (4.166664568298827e-2 + square * (-1.388731625493765e-3 + square * 2.443315711809948e-5))
    )
    quadrant = turns.astype(jnp.int32)
    swap = (quadrant & 1) == 1
    sine_out = jnp.where(swap, cosine, sine)
    cosine_out = jnp.where(swap, sine, cosine)
    sine_out = jnp.where((quadrant & 2) == 2, -sine_out, sine_out)
    cosine_out = jnp.where(((quadrant + 1) & 2) == 2, -cosine_out, cosine_out)
    return (cosine_out, sine_out)


def dot(left, right):
    return jnp.dot(left, right, preferred_element_type=F32)


def dot_t(left, right):
    return lax.dot_general(left, right, (((1,), (1,)), ((), ())), preferred_element_type=F32)


def columns(chunk):
    return slice(chunk * PAIR, (chunk + 1) * PAIR)


def centre_of(band_ref, pair):
    return jnp.concatenate([band_ref[half, pair, 0:BLOCK, :] for half in (0, 1)], axis=0)


def edge_of(band_ref, pair, side):
    cols = slice(side * BLOCK, (side + 1) * BLOCK)
    return jnp.concatenate([band_ref[half, pair, BLOCK:PIECE, cols] for half in (0, 1)], axis=0)


def rounded(value):
    return value.astype(BF16).astype(F32)


def band_kernel(half_ref, band_ref, out_ref):
    half = half_ref[0]
    rows = pl.ds(pl.multiple_of(half * (BLOCK // 2), BLOCK // 2), BLOCK // 2)
    centre = jnp.concatenate([band_ref[0, 1 + half], band_ref[1, half]], axis=1)
    edge = jnp.concatenate([band_ref[0, 0, rows, :], band_ref[1, 2, rows, :]], axis=1)
    for copy in range(out_ref.shape[0]):
        out_ref[copy, 0:BLOCK, :] = centre
        out_ref[copy, BLOCK:PIECE, :] = edge


def merge_kernel(half_ref, own_ref, other_ref, out_ref):
    half = half_ref[0]
    out_ref[half] = own_ref[...]
    out_ref[1 - half] = other_ref[...]


def copies_kernel(value_ref, out_ref):
    for copy in range(out_ref.shape[0]):
        out_ref[copy] = value_ref[...]


def phase(fields, cosine, sine):
    parts = []
    for member in range(fields.shape[0] // (2 * HALO)):
        base = member * 2 * HALO
        real, imag = (fields[base : base + HALO], fields[base + HALO : base + 2 * HALO])
        parts.append(real * cosine - imag * sine)
        parts.append(real * sine + imag * cosine)
    return jnp.concatenate(parts, axis=0)


def first_kernel(omega_ref, params_ref, fields_ref, rows_ref, phased_ref, angle_ref):
    omega = omega_ref[0]
    for chunk in range(params_ref.shape[3] // PAIR):
        cols = columns(chunk)
        cosine, sine = cos_sin(omega * params_ref[0, 0, :, cols])
        angle_ref[0:HALO, cols] = cosine
        angle_ref[HALO : 2 * HALO, cols] = sine
        phased = phase(fields_ref[:, cols].astype(F32), cosine, sine)
        phased_ref[:, cols] = phased
        rows_ref[:, cols] = phased.astype(BF16)


def middle_kernel(level, omega_ref, params_ref, band_ref, weights_ref, rows_ref, lateral_ref, *angle_refs):
    omega = omega_ref[0]
    pairs = band_ref.shape[1]
    height = rows_ref.shape[0]
    for pair in range(pairs):
        cols = columns(pair)
        rows = rows_ref[:, cols]
        total = dot(rows, centre_of(band_ref, pair))
        spread = dot(weights_ref[...], rows)
        total = total + (spread[:height] + spread[height:])
        zero = jnp.zeros((height, BLOCK), F32)
        left, right = (zero, zero)
        if pair > 0:
            before = rows_ref[:, pair * PAIR - BLOCK : pair * PAIR]
            left = dot(before, edge_of(band_ref, pair, 0))
        if pair < pairs - 1:
            after = rows_ref[:, (pair + 1) * PAIR : (pair + 1) * PAIR + BLOCK]
            right = dot(after, edge_of(band_ref, pair, 1))
        lateral_ref[:, cols] = total + jnp.concatenate([left, right], axis=1)
        if angle_refs:
            cosine, sine = cos_sin(omega * params_ref[level + 1, 0, :, cols])
            angle_refs[0][0:HALO, cols] = cosine
            angle_refs[0][HALO : 2 * HALO, cols] = sine


def sides(weights_ref, first_ref, second_ref, cols):
    both = jnp.concatenate([first_ref[:, cols], second_ref[:, cols]], axis=0)
    spread = dot(weights_ref[...], both)
    height = first_ref.shape[0]
    return spread[:height] + spread[height:]


def step_kernel(level, last, *refs):
    if last:
        params, weights, lateral, first, second, phased, state, product = refs
    else:
        params, weights, lateral, first, second, phased, angle = refs[:7]
        state, product, rows_next, phased_next = refs[7:]
    for chunk in range(params.shape[3] // PAIR):
        cols = columns(chunk)
        total = lateral[:, cols] + sides(weights, first, second, cols)
        coef = params[level, 1, :, cols]
        value = phased[:, cols]
        part = [slice(k * HALO, (k + 1) * HALO) for k in range(4)]
        source_re = value[part[0]] - coef * total[part[1]]
        source_im = value[part[1]] + coef * total[part[0]]
        receiver_re = value[part[2]] - coef * total[part[3]]
        receiver_im = value[part[3]] + coef * total[part[2]]
        state[0:HALO, cols] = source_re
        state[HALO : 2 * HALO, cols] = source_im
        product[:, cols] = source_re * receiver_re + source_im * receiver_im
        if not last:
            stepped = jnp.concatenate([source_re, source_im, receiver_re, receiver_im], axis=0)
            entering = stepped.astype(BF16).astype(F32)
            cosine, sine = (angle[0:HALO, cols], angle[HALO : 2 * HALO, cols])
            following = phase(entering, cosine, sine)
            phased_next[:, cols] = following
            rows_next[:, cols] = following.astype(BF16)


def image_kernel(parts_ref, mask_ref, image_ref, masked_ref):
    count = parts_ref.shape[0]
    total = parts_ref[0]
    for member in range(1, count):
        total = total + parts_ref[member]
    image = total / count
    image_ref[...] = image
    masked = mask_ref[...].astype(F32) * image
    for copy in range(count):
        masked_ref[copy] = masked


def gradient_kernel(parts_ref, gradient_ref):
    count = parts_ref.shape[0]
    total = parts_ref[0]
    for member in range(1, count):
        total = total + parts_ref[member]
    gradient_ref[...] = total / count


def scaled_rows(adjoint, coef):
    return jnp.concatenate([adjoint[:HALO] * coef, adjoint[HALO:] * coef], axis=0).astype(BF16)


def weighted(masked, state):
    return jnp.concatenate([masked * state[:HALO], masked * state[HALO:]], axis=0)


def adjoint_kernel(level, params, masked, state, adjoint, scaled):
    for chunk in range(params.shape[3] // PAIR):
        cols = columns(chunk)
        value = weighted(masked[level, :, cols], state[:, cols])
        adjoint[:, cols] = value
        scaled[:, cols] = scaled_rows(value, params[level, 1, :, cols])


def middle_back_kernel(band_ref, weights_ref, rows_ref, lateral_ref):
    pairs = band_ref.shape[1]
    height = rows_ref.shape[0]
    for pair in range(pairs):
        cols = columns(pair)
        rows = rows_ref[:, cols]
        total = dot_t(rows, centre_of(band_ref, pair))
        spread = dot(weights_ref[...], rows)
        total = total + (spread[:height] + spread[height:])
        zero = jnp.zeros((height, BLOCK), F32)
        left, right = (zero, zero)
        if pair > 0:
            before = rows_ref[:, pair * PAIR - BLOCK : pair * PAIR]
            left = dot_t(before, edge_of(band_ref, pair - 1, 1))
        if pair < pairs - 1:
            after = rows_ref[:, (pair + 1) * PAIR : (pair + 1) * PAIR + BLOCK]
            right = dot_t(after, edge_of(band_ref, pair + 1, 0))
        lateral_ref[:, cols] = total + jnp.concatenate([left, right], axis=1)


def back_kernel(level, last, *refs):
    if last:
        omega, params, weights, lateral, first, second, adjoint, phased, term = refs
    else:
        omega, params, weights, lateral, first, second, adjoint, phased = refs[:8]
        angle, masked, state, term, adjoint_next, scaled_next = refs[8:]
    for chunk in range(params.shape[3] // PAIR):
        cols = columns(chunk)
        total = lateral[:, cols] + sides(weights, first, second, cols)
        value = adjoint[:, cols]
        back_re = value[:HALO] + total[HALO:]
        back_im = value[HALO:] - total[:HALO]
        phase_re = phased[2 * HALO : 3 * HALO, cols]
        phase_im = phased[3 * HALO : 4 * HALO, cols]
        term[:, cols] = omega[0] * (back_im * phase_re - back_re * phase_im)
        if not last:
            cosine, sine = (angle[0:HALO, cols], angle[HALO : 2 * HALO, cols])
            upward = jnp.concatenate(
                [back_re * cosine + back_im * sine, back_im * cosine - back_re * sine], axis=0
            )
            upward = upward.astype(BF16).astype(F32)
            following = weighted(masked[level - 1, :, cols], state[:, cols]) + upward
            adjoint_next[:, cols] = following
            scaled_next[:, cols] = scaled_rows(following, params[level - 1, 1, :, cols])


def call(kernel, name, outs, cost, *args):
    placed = []
    for arg in args:
        scalar = arg.shape == (1,)
        placed.append(arg if scalar else pltpu.with_memory_space_constraint(arg, pltpu.VMEM))
    return pl.pallas_call(
        kernel,
        name=name,
        out_shape=[pltpu.VMEM(shape, kind) for shape, kind in outs],
        in_specs=[SMEM if arg.shape == (1,) else VMEM for arg in args],
        out_specs=[VMEM] * len(outs),
        cost_estimate=pl.CostEstimate(flops=cost, bytes_accessed=1 << 20, transcendentals=0),
        compiler_params=pltpu.CompilerParams(vmem_limit_bytes=8 << 20),
    )(*placed)


def stack_kernel(*refs):
    for index, ref in enumerate(refs[:-1]):
        refs[-1][index] = ref[...]


def stacked(parts):
    shape = (len(parts),) + parts[0].shape
    return call(stack_kernel, "stack", [(shape, F32)], 1000, *parts)[0]


def frequency_of(depth, lat, sections, size):
    upper = lat >= size // 2
    return (depth + upper * (sections // 2)) % sections


def home_of(row, size):
    half = size // 2
    return row if row < half else half + (row - half - 2) % half


def moved(value, inward=True):
    size = lax.axis_size("lat")
    route = [(row, home_of(row, size)) for row in range(size)]
    return lax.ppermute(value, "lat", route if inward else [(b, a) for a, b in route])


def swapped(rows):
    sections, size = (lax.axis_size("depth"), lax.axis_size("lat"))
    place = {}
    for row in range(size):
        lat = home_of(row, size)
        for depth in range(sections):
            place[frequency_of(depth, lat, sections, size), row] = depth * size + lat
    received = []
    for offset in (1, 0):
        route = []
        for member in range(sections):
            for row in range(offset, size - 1, 2):
                one, other = (place[member, row], place[member, row + 1])
                route += [(one, other), (other, one)]
        received.append(lax.ppermute(rows, ("depth", "lat"), route))
    return received


def exchanged(parts):
    return lax.all_to_all(parts, "depth", 0, 0)


def per_device(source_field, receiver_field, freq_index, slowness, ffd_coef, band, image_mask):
    sections = lax.axis_size("depth")
    lat, size = (lax.axis_index("lat"), lax.axis_size("lat"))
    member = frequency_of(lax.axis_index("depth"), lat, sections, size)
    height, width = slowness.shape[1:]
    levels = sections
    omega = 0.1 * (lax.dynamic_slice_in_dim(freq_index, member, 1).astype(F32) + 1.0)
    odd = lax.rem(lat, 2)
    side_fore = jnp.where(odd == 1, *side_weights(4)[::-1])
    side_back = jnp.where(odd == 1, *side_weights(2)[::-1])
    own_fore, own_back = (jnp.asarray(own_weights(4)), jnp.asarray(own_weights(2)))
    source = lax.dynamic_index_in_dim(source_field, member, 0, keepdims=False)
    receiver = lax.dynamic_index_in_dim(receiver_field, member, 0, keepdims=False)
    fields = jnp.concatenate([source, receiver]).reshape(4 * height, width)

    wide, half, single = ((4 * height, width), (2 * height, width), (height, width))
    own = moved(jnp.stack([slowness[0], ffd_coef[0]]))
    fields = moved(fields)
    mask = moved(image_mask[0])
    half_index = odd.astype(jnp.int32).reshape(1)
    (pieces,) = call(
        band_kernel, "band", [((sections, PIECE, PAIR), BF16)], 1000, half_index, band
    )
    pieces = exchanged(pieces)
    (params,) = call(copies_kernel, "copies", [((sections, 2) + single, F32)], 1000, own)
    pieces, _ = lax.optimization_barrier((pieces, params))
    params = exchanged(params)
    route = [(lat, lat + 1 - lat % 2 * 2) for lat in range(size)]
    other = lax.ppermute(pieces, "lat", route)
    (band,) = call(
        merge_kernel, "merge", [((2,) + pieces.shape, BF16)], 1000, half_index, pieces, other
    )
    rows, phased, angle = call(
        first_kernel, "first", [(wide, BF16), (wide, F32), (half, F32)], 1000, omega, params, fields
    )
    states, products, phases, angles = ([], [], [phased], [angle])
    for level in range(levels):
        last = level == levels - 1
        first, second = swapped(rows)
        outs = [(wide, F32)] + ([] if last else [(half, F32)])
        lateral, *more = call(
            functools.partial(middle_kernel, level),
            "middle",
            outs,
            1 << 28,
            omega,
            params,
            band,
            own_fore,
            rows,
        )
        angles += more
        outs = [(half, F32), (single, F32)] + ([] if last else [(wide, BF16), (wide, F32)])
        args = [params, side_fore, lateral, first, second, phased] + more
        state, product, *more = call(
            functools.partial(step_kernel, level, last), "step", outs, 1 << 20, *args
        )
        states.append(state)
        products.append(product)
        if not last:
            rows, phased = more
            phases.append(phased)

    image, masked = call(
        image_kernel,
        "image",
        [(single, F32), ((sections,) + single, F32)],
        1000,
        exchanged(stacked(products)),
        mask,
    )
    masked = exchanged(masked)
    image = moved(image, False)

    level = levels - 1
    adjoint, scaled = call(
        functools.partial(adjoint_kernel, level),
        "adjoint",
        [(half, F32), (half, BF16)],
        1000,
        params,
        masked,
        states[level],
    )
    terms = [None] * levels
    for level in reversed(range(levels)):
        last = level == 0
        first, second = swapped(scaled)
        (lateral,) = call(
            middle_back_kernel, "middle_back", [(half, F32)], 1 << 28, band, own_back, scaled
        )
        args = [omega, params, side_back, lateral, first, second, adjoint, phases[level]]
        outs = [(single, F32)]
        if not last:
            args += [angles[level], masked, states[level - 1]]
            outs += [(half, F32), (half, BF16)]
        terms[level], *more = call(
            functools.partial(back_kernel, level, last), "back", outs, 1 << 20, *args
        )
        if not last:
            adjoint, scaled = more
    (gradient,) = call(
        gradient_kernel, "gradient", [(single, F32)], 1000, exchanged(stacked(terms))
    )
    return (image[None], moved(gradient, False)[None])


def solution(mesh):
    return jax.shard_map(
        per_device,
        mesh=mesh,
        in_specs=(
            P(None, None, "lat", None),
            P(None, None, "lat", None),
            P(),
            P("depth", "lat", None),
            P("depth", "lat", None),
            P("depth", None, None, None),
            P("depth", "lat", None),
        ),
        out_specs=(P("depth", "lat", None), P("depth", "lat", None)),
        check_vma=False,
    )
```

```python
import functools
import jax
import jax.numpy as jnp
import numpy as np
from jax import lax
from jax.experimental import pallas as pl
from jax.experimental.pallas import tpu as pltpu
from jax.sharding import PartitionSpec as P

HALO = 8
BLOCK = 128
PAIR = 2 * BLOCK
PIECE = BLOCK + BLOCK // 2
VMEM = pl.BlockSpec(memory_space=pltpu.VMEM)
SMEM = pl.BlockSpec(memory_space=pltpu.SMEM)
F32, BF16 = jnp.float32, jnp.bfloat16


def stencil_weight(distance):
    if distance == 0:
        return sum(-0.5 / k for k in range(1, HALO + 1))
    return 0.25 / abs(distance) if abs(distance) <= HALO else 0.0


def stencil_matrix(combos, shift):
    small = np.zeros((HALO, HALO))
    for row in range(HALO):
        for source in range(HALO):
            small[row, source] = stencil_weight(shift + source - row)
    return np.kron(np.eye(combos), small)


def split_weights(matrix):
    high = matrix.astype(jnp.bfloat16)
    low = (matrix - high.astype(np.float64)).astype(jnp.bfloat16)
    return np.concatenate([high, low], axis=0)


def own_weights(combos):
    return split_weights(stencil_matrix(combos, 0))


def side_weights(combos):
    after, before = (stencil_matrix(combos, HALO), stencil_matrix(combos, -HALO))
    even = split_weights(np.concatenate([before, after], axis=1))
    odd = split_weights(np.concatenate([after, before], axis=1))
    return np.stack([even, odd])


def cos_sin(theta):
    turns = jnp.floor(theta * 0.6366197723675814 + 0.5)
    rest = theta - turns * 1.5703125
    rest = rest - turns * 4.837512969970703e-4
    rest = rest - turns * 7.549789948768648e-8
    square = rest * rest
    sine = rest + rest * square * (
        -1.6666654611e-1 + square * (8.3321608736e-3 + square * -1.9515295891e-4)
    )
    cosine = (
        1.0
        - 0.5 * square
        + square
        * square
        * (4.166664568298827e-2 + square * (-1.388731625493765e-3 + square * 2.443315711809948e-5))
    )
    quadrant = turns.astype(jnp.int32)
    swap = (quadrant & 1) == 1
    sine_out = jnp.where(swap, cosine, sine)
    cosine_out = jnp.where(swap, sine, cosine)
    sine_out = jnp.where((quadrant & 2) == 2, -sine_out, sine_out)
    cosine_out = jnp.where(((quadrant + 1) & 2) == 2, -cosine_out, cosine_out)
    return (cosine_out, sine_out)


def dot(left, right):
    return jnp.dot(left, right, preferred_element_type=F32)


def dot_t(left, right):
    return lax.dot_general(left, right, (((1,), (1,)), ((), ())), preferred_element_type=F32)


def columns(chunk):
    return slice(chunk * PAIR, (chunk + 1) * PAIR)


def centre_of(band_ref, pair):
    return jnp.concatenate([band_ref[half, pair, 0:BLOCK, :] for half in (0, 1)], axis=0)


def edge_of(band_ref, pair, side):
    cols = slice(side * BLOCK, (side + 1) * BLOCK)
    return jnp.concatenate([band_ref[half, pair, BLOCK:PIECE, cols] for half in (0, 1)], axis=0)


def band_kernel(half_ref, band_ref, out_ref):
    half = half_ref[0]
    rows = pl.ds(pl.multiple_of(half * (BLOCK // 2), BLOCK // 2), BLOCK // 2)
    centre = jnp.concatenate([band_ref[0, 1 + half], band_ref[1, half]], axis=1)
    edge = jnp.concatenate([band_ref[0, 0, rows, :], band_ref[1, 2, rows, :]], axis=1)
    for copy in range(out_ref.shape[0]):
        out_ref[copy, 0:BLOCK, :] = centre
        out_ref[copy, BLOCK:PIECE, :] = edge


def merge_kernel(half_ref, own_ref, other_ref, out_ref):
    half = half_ref[0]
    out_ref[half] = own_ref[...]
    out_ref[1 - half] = other_ref[...]


def copies_kernel(value_ref, out_ref):
    for copy in range(out_ref.shape[0]):
        out_ref[copy] = value_ref[...]


def coef_of(params, level, cols):
    return jnp.abs(params[level, 1, :, cols])


def visible(params, level, cols, image):
    return jnp.where(params[level, 1, :, cols] > 0.0, image, 0.0)


def phase(fields, cosine, sine):
    parts = []
    for member in range(fields.shape[0] // (2 * HALO)):
        base = member * 2 * HALO
        real, imag = (fields[base : base + HALO], fields[base + HALO : base + 2 * HALO])
        parts.append(real * cosine - imag * sine)
        parts.append(real * sine + imag * cosine)
    return jnp.concatenate(parts, axis=0)


def first_kernel(omega_ref, params_ref, fields_ref, rows_ref, phased_ref, angle_ref):
    omega = omega_ref[0]
    for chunk in range(params_ref.shape[3] // PAIR):
        cols = columns(chunk)
        cosine, sine = cos_sin(omega * params_ref[0, 0, :, cols])
        angle_ref[0:HALO, cols] = cosine
        angle_ref[HALO : 2 * HALO, cols] = sine
        phased = phase(fields_ref[:, cols].astype(F32), cosine, sine)
        phased_ref[:, cols] = phased
        rows_ref[:, cols] = phased.astype(BF16)


def middle_kernel(level, omega_ref, params_ref, band_ref, weights_ref, rows_ref, lateral_ref, *angle_refs):
    omega = omega_ref[0]
    pairs = band_ref.shape[1]
    height = rows_ref.shape[0]
    for pair in range(pairs):
        cols = columns(pair)
        rows = rows_ref[:, cols]
        total = dot(rows, centre_of(band_ref, pair))
        spread = dot(weights_ref[...], rows)
        total = total + (spread[:height] + spread[height:])
        zero = jnp.zeros((height, BLOCK), F32)
        left, right = (zero, zero)
        if pair > 0:
            before = rows_ref[:, pair * PAIR - BLOCK : pair * PAIR]
            left = dot(before, edge_of(band_ref, pair, 0))
        if pair < pairs - 1:
            after = rows_ref[:, (pair + 1) * PAIR : (pair + 1) * PAIR + BLOCK]
            right = dot(after, edge_of(band_ref, pair, 1))
        lateral_ref[:, cols] = total + jnp.concatenate([left, right], axis=1)
        if angle_refs:
            cosine, sine = cos_sin(omega * params_ref[level + 1, 0, :, cols])
            angle_refs[0][0:HALO, cols] = cosine
            angle_refs[0][HALO : 2 * HALO, cols] = sine


def sides(weights_ref, first_ref, second_ref, cols):
    both = jnp.concatenate([first_ref[:, cols], second_ref[:, cols]], axis=0)
    spread = dot(weights_ref[...], both)
    height = first_ref.shape[0]
    return spread[:height] + spread[height:]


def step_kernel(level, last, *refs):
    params, weights, lateral, first, second, phased = refs[:6]
    if last:
        state, products = refs[-2:]
    else:
        angle = refs[6]
        state, products, rows_next, phased_next = refs[-4:]
    halves = products.shape[2] // PAIR
    for index in range(halves):
        pieces = []
        for chunk in (index, index + halves):
            cols = columns(chunk)
            total = lateral[:, cols] + sides(weights, first, second, cols)
            coef = coef_of(params, level, cols)
            value = phased[:, cols]
            part = [slice(k * HALO, (k + 1) * HALO) for k in range(4)]
            source_re = value[part[0]] - coef * total[part[1]]
            source_im = value[part[1]] + coef * total[part[0]]
            receiver_re = value[part[2]] - coef * total[part[3]]
            receiver_im = value[part[3]] + coef * total[part[2]]
            state[0:HALO, cols] = source_re
            state[HALO : 2 * HALO, cols] = source_im
            pieces.append(source_re * receiver_re + source_im * receiver_im)
            if not last:
                stepped = jnp.concatenate(
                    [source_re, source_im, receiver_re, receiver_im], axis=0
                )
                entering = stepped.astype(BF16).astype(F32)
                cosine, sine = (angle[0:HALO, cols], angle[HALO : 2 * HALO, cols])
                following = phase(entering, cosine, sine)
                phased_next[:, cols] = following
                rows_next[:, cols] = following.astype(BF16)
        products[level, :, columns(index)] = jnp.concatenate(pieces, axis=0).astype(BF16)


def mean_of(parts_ref, cols):
    count = parts_ref.shape[0]
    total = parts_ref[0, :, cols].astype(F32)
    for member in range(1, count):
        total = total + parts_ref[member, :, cols].astype(F32)
    return total / count


def image_kernel(parts_ref, image_ref, copies_ref):
    halves = parts_ref.shape[2] // PAIR
    for index in range(halves):
        cols = columns(index)
        image = mean_of(parts_ref, cols)
        image_ref[:, cols] = image[:HALO]
        image_ref[:, columns(index + halves)] = image[HALO:]
        for copy in range(copies_ref.shape[0]):
            copies_ref[copy, :, cols] = image.astype(BF16)


def gradient_kernel(parts_ref, gradient_ref):
    halves = parts_ref.shape[2] // PAIR
    for index in range(halves):
        gradient = mean_of(parts_ref, columns(index))
        gradient_ref[:, columns(index)] = gradient[:HALO]
        gradient_ref[:, columns(index + halves)] = gradient[HALO:]


def scaled_rows(adjoint, coef):
    return jnp.concatenate([adjoint[:HALO] * coef, adjoint[HALO:] * coef], axis=0).astype(BF16)


def weighted(masked, state):
    return jnp.concatenate([masked * state[:HALO], masked * state[HALO:]], axis=0)


def adjoint_kernel(level, params, images, state, adjoint, scaled):
    halves = images.shape[2] // PAIR
    for index in range(halves):
        image = images[level, :, columns(index)].astype(F32)
        for chunk, part in ((index, image[:HALO]), (index + halves, image[HALO:])):
            cols = columns(chunk)
            value = weighted(visible(params, level, cols, part), state[:, cols])
            adjoint[:, cols] = value
            scaled[:, cols] = scaled_rows(value, coef_of(params, level, cols))


def middle_back_kernel(band_ref, weights_ref, rows_ref, lateral_ref):
    pairs = band_ref.shape[1]
    height = rows_ref.shape[0]
    for pair in range(pairs):
        cols = columns(pair)
        rows = rows_ref[:, cols]
        total = dot_t(rows, centre_of(band_ref, pair))
        spread = dot(weights_ref[...], rows)
        total = total + (spread[:height] + spread[height:])
        zero = jnp.zeros((height, BLOCK), F32)
        left, right = (zero, zero)
        if pair > 0:
            before = rows_ref[:, pair * PAIR - BLOCK : pair * PAIR]
            left = dot_t(before, edge_of(band_ref, pair - 1, 1))
        if pair < pairs - 1:
            after = rows_ref[:, (pair + 1) * PAIR : (pair + 1) * PAIR + BLOCK]
            right = dot_t(after, edge_of(band_ref, pair + 1, 0))
        lateral_ref[:, cols] = total + jnp.concatenate([left, right], axis=1)


def back_kernel(level, last, *refs):
    omega, params, weights, lateral, first, second, adjoint, phased = refs[:8]
    if last:
        term = refs[-1].at[0]
        for later, ref in enumerate(refs[8:-1]):
            refs[-1][later + 1] = ref[...]
    else:
        angle, images, state, term, adjoint_next, scaled_next = refs[8:]
    halves = term.shape[1] // PAIR
    for index in range(halves):
        pieces = []
        if not last:
            image = images[level - 1, :, columns(index)].astype(F32)
        for place, chunk in enumerate((index, index + halves)):
            cols = columns(chunk)
            total = lateral[:, cols] + sides(weights, first, second, cols)
            value = adjoint[:, cols]
            back_re = value[:HALO] + total[HALO:]
            back_im = value[HALO:] - total[:HALO]
            phase_re = phased[2 * HALO : 3 * HALO, cols]
            phase_im = phased[3 * HALO : 4 * HALO, cols]
            pieces.append(omega[0] * (back_im * phase_re - back_re * phase_im))
            if not last:
                cosine, sine = (angle[0:HALO, cols], angle[HALO : 2 * HALO, cols])
                upward = jnp.concatenate(
                    [back_re * cosine + back_im * sine, back_im * cosine - back_re * sine],
                    axis=0,
                )
                upward = upward.astype(BF16).astype(F32)
                part = image[place * HALO : (place + 1) * HALO]
                masked = visible(params, level - 1, cols, part)
                following = weighted(masked, state[:, cols]) + upward
                adjoint_next[:, cols] = following
                scaled_next[:, cols] = scaled_rows(following, coef_of(params, level - 1, cols))
        term[:, columns(index)] = jnp.concatenate(pieces, axis=0).astype(BF16)


def call(kernel, name, outs, cost, *args, reuse=None):
    placed = []
    for arg in args:
        scalar = arg.shape == (1,)
        placed.append(arg if scalar else pltpu.with_memory_space_constraint(arg, pltpu.VMEM))
    return pl.pallas_call(
        kernel,
        name=name,
        out_shape=[pltpu.VMEM(shape, kind) for shape, kind in outs],
        in_specs=[SMEM if arg.shape == (1,) else VMEM for arg in args],
        out_specs=[VMEM] * len(outs),
        input_output_aliases=reuse or {},
        cost_estimate=pl.CostEstimate(flops=cost, bytes_accessed=1 << 20, transcendentals=0),
        compiler_params=pltpu.CompilerParams(vmem_limit_bytes=8 << 20),
    )(*placed)


def frequency_of(depth, lat, sections, size):
    upper = lat >= size // 2
    return (depth + upper * (sections // 2)) % sections


def home_of(row, size):
    half = size // 2
    return row if row < half else half + (row - half - 2) % half


def moved(value, inward=True):
    size = lax.axis_size("lat")
    route = [(row, home_of(row, size)) for row in range(size)]
    return lax.ppermute(value, "lat", route if inward else [(b, a) for a, b in route])


def swapped(rows):
    sections, size = (lax.axis_size("depth"), lax.axis_size("lat"))
    place = {}
    for row in range(size):
        lat = home_of(row, size)
        for depth in range(sections):
            place[frequency_of(depth, lat, sections, size), row] = depth * size + lat
    received = []
    for offset in (1, 0):
        route = []
        for member in range(sections):
            for row in range(offset, size - 1, 2):
                one, other = (place[member, row], place[member, row + 1])
                route += [(one, other), (other, one)]
        received.append(lax.ppermute(rows, ("depth", "lat"), route))
    return received


def exchanged(parts):
    return lax.all_to_all(parts, "depth", 0, 0)


def per_device(source_field, receiver_field, freq_index, slowness, ffd_coef, band, image_mask):
    sections = lax.axis_size("depth")
    lat, size = (lax.axis_index("lat"), lax.axis_size("lat"))
    member = frequency_of(lax.axis_index("depth"), lat, sections, size)
    height, width = slowness.shape[1:]
    levels = sections
    omega = 0.1 * (lax.dynamic_slice_in_dim(freq_index, member, 1).astype(F32) + 1.0)
    odd = lax.rem(lat, 2)
    side_fore = jnp.where(odd == 1, *side_weights(4)[::-1])
    side_back = jnp.where(odd == 1, *side_weights(2)[::-1])
    own_fore, own_back = (jnp.asarray(own_weights(4)), jnp.asarray(own_weights(2)))
    source = lax.dynamic_index_in_dim(source_field, member, 0, keepdims=False)
    receiver = lax.dynamic_index_in_dim(receiver_field, member, 0, keepdims=False)
    fields = jnp.concatenate([source, receiver]).reshape(4 * height, width)

    wide, half, single = ((4 * height, width), (2 * height, width), (height, width))
    signed = jnp.where(image_mask[0] > 0, ffd_coef[0], -ffd_coef[0])
    own = moved(jnp.stack([slowness[0], signed]))
    fields = moved(fields)
    half_index = odd.astype(jnp.int32).reshape(1)
    (pieces,) = call(
        band_kernel, "band", [((sections, PIECE, PAIR), BF16)], 1000, half_index, band
    )
    pieces = exchanged(pieces)
    (params,) = call(copies_kernel, "copies", [((sections, 2) + single, F32)], 1000, own)
    pieces, _ = lax.optimization_barrier((pieces, params))
    params = exchanged(params)
    route = [(lat, lat + 1 - lat % 2 * 2) for lat in range(size)]
    other = lax.ppermute(pieces, "lat", route)
    (band,) = call(
        merge_kernel, "merge", [((2,) + pieces.shape, BF16)], 1000, half_index, pieces, other
    )
    rows, phased, angle = call(
        first_kernel, "first", [(wide, BF16), (wide, F32), (half, F32)], 1000, omega, params, fields
    )
    folded = (sections, 2 * height, width // 2)
    states, phases, angles = ([], [phased], [angle])
    products = []
    for level in range(levels):
        last = level == levels - 1
        first, second = swapped(rows)
        outs = [(wide, F32)] + ([] if last else [(half, F32)])
        lateral, *more = call(
            functools.partial(middle_kernel, level),
            "middle",
            outs,
            1 << 28,
            omega,
            params,
            band,
            own_fore,
            rows,
        )
        angles += more
        outs = [(half, F32), (folded, BF16)]
        outs += [] if last else [(wide, BF16), (wide, F32)]
        args = [params, side_fore, lateral, first, second, phased] + more + products
        state, products, *more = call(
            functools.partial(step_kernel, level, last),
            "step",
            outs,
            1 << 20,
            *args,
            reuse={len(args) - 1: 1} if products else None,
        )
        products = [products]
        states.append(state)
        if not last:
            rows, phased = more
            phases.append(phased)

    image, images = call(
        image_kernel, "image", [(single, F32), (folded, BF16)], 1000, exchanged(products[0])
    )
    images = exchanged(images)
    image = moved(image, False)

    level = levels - 1
    adjoint, scaled = call(
        functools.partial(adjoint_kernel, level),
        "adjoint",
        [(half, F32), (half, BF16)],
        1000,
        params,
        images,
        states[level],
    )
    terms = []
    for level in reversed(range(levels)):
        last = level == 0
        first, second = swapped(scaled)
        (lateral,) = call(
            middle_back_kernel, "middle_back", [(half, F32)], 1 << 28, band, own_back, scaled
        )
        args = [omega, params, side_back, lateral, first, second, adjoint, phases[level]]
        if last:
            args += terms
            outs = [(folded, BF16)]
        else:
            args += [angles[level], images, states[level - 1]]
            outs = [(folded[1:], BF16), (half, F32), (half, BF16)]
        term, *more = call(
            functools.partial(back_kernel, level, last),
            "back",
            outs,
            1 << 20,
            *args,
        )
        terms = [term] + terms
        if not last:
            adjoint, scaled = more
    (gradient,) = call(
        gradient_kernel, "gradient", [(single, F32)], 1000, exchanged(terms[0])
    )
    return (image[None], moved(gradient, False)[None])


def solution(mesh):
    return jax.shard_map(
        per_device,
        mesh=mesh,
        in_specs=(
            P(None, None, "lat", None),
            P(None, None, "lat", None),
            P(),
            P("depth", "lat", None),
            P("depth", "lat", None),
            P("depth", None, None, None),
            P("depth", "lat", None),
        ),
        out_specs=(P("depth", "lat", None), P("depth", "lat", None)),
        check_vma=False,
    )
```

```python
import functools
import jax
import jax.numpy as jnp
import numpy as np
from jax import lax
from jax.experimental import pallas as pl
from jax.experimental.pallas import tpu as pltpu
from jax.sharding import PartitionSpec as P

HALO = 8
BLOCK = 128
PAIR = 2 * BLOCK
VMEM = pl.BlockSpec(memory_space=pltpu.VMEM)
SMEM = pl.BlockSpec(memory_space=pltpu.SMEM)
F32, BF16 = jnp.float32, jnp.bfloat16


def stencil_weight(distance):
    if distance == 0:
        return sum(-0.5 / k for k in range(1, HALO + 1))
    return 0.25 / abs(distance) if abs(distance) <= HALO else 0.0


def stencil_matrix(combos, shift):
    small = np.zeros((HALO, HALO))
    for row in range(HALO):
        for source in range(HALO):
            small[row, source] = stencil_weight(shift + source - row)
    return np.kron(np.eye(combos), small)


def split_weights(matrix):
    high = matrix.astype(jnp.bfloat16)
    low = (matrix - high.astype(np.float64)).astype(jnp.bfloat16)
    return np.concatenate([high, low], axis=0)


def weights_of(combos):
    own, after, before = [stencil_matrix(combos, shift) for shift in (0, HALO, -HALO)]
    even = np.concatenate([before, after, own], axis=1)
    odd = np.concatenate([after, before, own], axis=1)
    return [split_weights(matrix) for matrix in (even, odd)]


def cos_sin(theta):
    turns = jnp.floor(theta * 0.6366197723675814 + 0.5)
    rest = theta - turns * 1.5703125
    rest = rest - turns * 4.837512969970703e-4
    rest = rest - turns * 7.549789948768648e-8
    square = rest * rest
    sine = rest + rest * square * (
        -1.6666654611e-1 + square * (8.3321608736e-3 + square * -1.9515295891e-4)
    )
    cosine = (
        1.0
        - 0.5 * square
        + square
        * square
        * (4.166664568298827e-2 + square * (-1.388731625493765e-3 + square * 2.443315711809948e-5))
    )
    quadrant = turns.astype(jnp.int32)
    swap = (quadrant & 1) == 1
    sine_out = jnp.where(swap, cosine, sine)
    cosine_out = jnp.where(swap, sine, cosine)
    sine_out = jnp.where((quadrant & 2) == 2, -sine_out, sine_out)
    cosine_out = jnp.where(((quadrant + 1) & 2) == 2, -cosine_out, cosine_out)
    return (cosine_out, sine_out)


def dot(left, right):
    return jnp.dot(left, right, preferred_element_type=F32)


def dot_t(left, right):
    return lax.dot_general(left, right, (((1,), (1,)), ((), ())), preferred_element_type=F32)


def columns(chunk):
    return slice(chunk * PAIR, (chunk + 1) * PAIR)


def block_of(band_ref, index, offset):
    pair, place = (index // 2, index % 2)
    return jnp.concatenate([band_ref[half, pair, place, offset] for half in (0, 1)], axis=0)


def centre_of(band_ref, pair):
    first, second = (2 * pair, 2 * pair + 1)
    upper = [block_of(band_ref, first, 1), block_of(band_ref, second, 0)]
    lower = [block_of(band_ref, first, 2), block_of(band_ref, second, 1)]
    return jnp.concatenate(
        [jnp.concatenate(upper, axis=1), jnp.concatenate(lower, axis=1)], axis=0
    )


def edge_of(band_ref, pair, side):
    return block_of(band_ref, 2 * pair + side, 2 * side)


def merge_kernel(half_ref, own_ref, other_ref, out_ref):
    half = half_ref[0]
    out_ref[half] = own_ref[...]
    out_ref[1 - half] = other_ref[...]


def copies_kernel(value_ref, out_ref):
    for copy in range(out_ref.shape[0]):
        out_ref[copy] = value_ref[...]


def coef_of(params, level, cols):
    return jnp.abs(params[level, 1, :, cols])


def visible(params, level, cols, image):
    return jnp.where(params[level, 1, :, cols] > 0.0, image, 0.0)


def phase(fields, cosine, sine):
    parts = []
    for member in range(fields.shape[0] // (2 * HALO)):
        base = member * 2 * HALO
        real, imag = (fields[base : base + HALO], fields[base + HALO : base + 2 * HALO])
        parts.append(real * cosine - imag * sine)
        parts.append(real * sine + imag * cosine)
    return jnp.concatenate(parts, axis=0)


def first_kernel(omega_ref, params_ref, source_ref, receiver_ref, rows_ref, phased_ref, angle_ref):
    omega = omega_ref[0]
    for chunk in range(params_ref.shape[3] // PAIR):
        cols = columns(chunk)
        cosine, sine = cos_sin(omega * params_ref[0, 0, :, cols])
        angle_ref[0:HALO, cols] = cosine
        angle_ref[HALO : 2 * HALO, cols] = sine
        fields = jnp.concatenate([source_ref[:, cols], receiver_ref[:, cols]], axis=0)
        phased = phase(fields.astype(F32), cosine, sine)
        phased_ref[:, cols] = phased
        rows_ref[:, cols] = phased.astype(BF16)


def middle_kernel(level, omega_ref, params_ref, band_ref, weights_ref, rows_ref, lateral_ref, *angle_refs):
    omega = omega_ref[0]
    pairs = band_ref.shape[1]
    height = rows_ref.shape[0]
    for pair in range(pairs):
        cols = columns(pair)
        rows = rows_ref[:, cols]
        total = dot(rows, centre_of(band_ref, pair))
        spread = dot(weights_ref[:, 2 * height : 3 * height], rows)
        total = total + (spread[:height] + spread[height:])
        zero = jnp.zeros((height, BLOCK), F32)
        left, right = (zero, zero)
        if pair > 0:
            before = rows_ref[:, pair * PAIR - BLOCK : pair * PAIR]
            left = dot(before, edge_of(band_ref, pair, 0))
        if pair < pairs - 1:
            after = rows_ref[:, (pair + 1) * PAIR : (pair + 1) * PAIR + BLOCK]
            right = dot(after, edge_of(band_ref, pair, 1))
        lateral_ref[:, cols] = total + jnp.concatenate([left, right], axis=1)
        if angle_refs:
            cosine, sine = cos_sin(omega * params_ref[level + 1, 0, :, cols])
            angle_refs[0][0:HALO, cols] = cosine
            angle_refs[0][HALO : 2 * HALO, cols] = sine


def sides(weights_ref, first_ref, second_ref, cols):
    both = jnp.concatenate([first_ref[:, cols], second_ref[:, cols]], axis=0)
    height = first_ref.shape[0]
    spread = dot(weights_ref[:, 0 : 2 * height], both)
    return spread[:height] + spread[height:]


def step_kernel(level, last, *refs):
    params, weights, lateral, first, second, phased = refs[:6]
    if last:
        state, products = refs[-2:]
    else:
        angle = refs[6]
        state, products, rows_next, phased_next = refs[-4:]
    halves = params.shape[3] // PAIR // 2
    for index in range(halves):
        for chunk in (index, index + halves):
            cols = columns(chunk)
            total = lateral[:, cols] + sides(weights, first, second, cols)
            coef = coef_of(params, level, cols)
            value = phased[:, cols]
            part = [slice(k * HALO, (k + 1) * HALO) for k in range(4)]
            source_re = value[part[0]] - coef * total[part[1]]
            source_im = value[part[1]] + coef * total[part[0]]
            receiver_re = value[part[2]] - coef * total[part[3]]
            receiver_im = value[part[3]] + coef * total[part[2]]
            state[0:HALO, cols] = source_re
            state[HALO : 2 * HALO, cols] = source_im
            product = source_re * receiver_re + source_im * receiver_im
            if not last:
                stepped = jnp.concatenate(
                    [source_re, source_im, receiver_re, receiver_im], axis=0
                )
                entering = stepped.astype(BF16).astype(F32)
                cosine, sine = (angle[0:HALO, cols], angle[HALO : 2 * HALO, cols])
                following = phase(entering, cosine, sine)
                phased_next[:, cols] = following
                rows_next[:, cols] = following.astype(BF16)
            products[level, :, cols] = product


def mean_of(parts_ref, cols):
    count = parts_ref.shape[0]
    total = parts_ref[0, :, cols].astype(F32)
    for member in range(1, count):
        total = total + parts_ref[member, :, cols].astype(F32)
    return total / count


def image_kernel(parts_ref, image_ref, copies_ref):
    for chunk in range(parts_ref.shape[2] // PAIR):
        cols = columns(chunk)
        image = mean_of(parts_ref, cols)
        image_ref[:, cols] = image
        for copy in range(copies_ref.shape[0]):
            copies_ref[copy, :, cols] = image


def gradient_kernel(parts_ref, gradient_ref):
    halves = parts_ref.shape[2] // PAIR
    for index in range(halves):
        gradient = mean_of(parts_ref, columns(index))
        gradient_ref[:, columns(index)] = gradient[:HALO]
        gradient_ref[:, columns(index + halves)] = gradient[HALO:]


def scaled_rows(adjoint, coef):
    return jnp.concatenate([adjoint[:HALO] * coef, adjoint[HALO:] * coef], axis=0).astype(BF16)


def weighted(masked, state):
    return jnp.concatenate([masked * state[:HALO], masked * state[HALO:]], axis=0)


def adjoint_kernel(level, params, images, state, adjoint, scaled):
    for chunk in range(images.shape[2] // PAIR):
        cols = columns(chunk)
        masked = visible(params, level, cols, images[level, :, cols])
        value = weighted(masked, state[:, cols])
        adjoint[:, cols] = value
        scaled[:, cols] = scaled_rows(value, coef_of(params, level, cols))


def middle_back_kernel(band_ref, weights_ref, rows_ref, lateral_ref):
    pairs = band_ref.shape[1]
    height = rows_ref.shape[0]
    for pair in range(pairs):
        cols = columns(pair)
        rows = rows_ref[:, cols]
        total = dot_t(rows, centre_of(band_ref, pair))
        spread = dot(weights_ref[:, 2 * height : 3 * height], rows)
        total = total + (spread[:height] + spread[height:])
        zero = jnp.zeros((height, BLOCK), F32)
        left, right = (zero, zero)
        if pair > 0:
            before = rows_ref[:, pair * PAIR - BLOCK : pair * PAIR]
            left = dot_t(before, edge_of(band_ref, pair - 1, 1))
        if pair < pairs - 1:
            after = rows_ref[:, (pair + 1) * PAIR : (pair + 1) * PAIR + BLOCK]
            right = dot_t(after, edge_of(band_ref, pair + 1, 0))
        lateral_ref[:, cols] = total + jnp.concatenate([left, right], axis=1)


def back_kernel(level, last, *refs):
    omega, params, weights, lateral, first, second, adjoint, phased = refs[:8]
    if last:
        term = refs[-1].at[0]
        for later, ref in enumerate(refs[8:-1]):
            refs[-1][later + 1] = ref[...]
    else:
        angle, images, state, term, adjoint_next, scaled_next = refs[8:]
    halves = term.shape[1] // PAIR
    for index in range(halves):
        pieces = []
        for chunk in (index, index + halves):
            cols = columns(chunk)
            total = lateral[:, cols] + sides(weights, first, second, cols)
            value = adjoint[:, cols]
            back_re = value[:HALO] + total[HALO:]
            back_im = value[HALO:] - total[:HALO]
            phase_re = phased[2 * HALO : 3 * HALO, cols]
            phase_im = phased[3 * HALO : 4 * HALO, cols]
            pieces.append(omega[0] * (back_im * phase_re - back_re * phase_im))
            if not last:
                cosine, sine = (angle[0:HALO, cols], angle[HALO : 2 * HALO, cols])
                upward = jnp.concatenate(
                    [back_re * cosine + back_im * sine, back_im * cosine - back_re * sine],
                    axis=0,
                )
                upward = upward.astype(BF16).astype(F32)
                masked = visible(params, level - 1, cols, images[level - 1, :, cols])
                following = weighted(masked, state[:, cols]) + upward
                adjoint_next[:, cols] = following
                scaled_next[:, cols] = scaled_rows(following, coef_of(params, level - 1, cols))
        term[:, columns(index)] = jnp.concatenate(pieces, axis=0).astype(BF16)


def call(kernel, name, outs, cost, *args, reuse=None):
    placed = []
    for arg in args:
        scalar = arg.shape == (1,)
        placed.append(arg if scalar else pltpu.with_memory_space_constraint(arg, pltpu.VMEM))
    return pl.pallas_call(
        kernel,
        name=name,
        out_shape=[pltpu.VMEM(shape, kind) for shape, kind in outs],
        in_specs=[SMEM if arg.shape == (1,) else VMEM for arg in args],
        out_specs=[VMEM] * len(outs),
        input_output_aliases=reuse or {},
        cost_estimate=pl.CostEstimate(flops=cost, bytes_accessed=1 << 20, transcendentals=0),
        compiler_params=pltpu.CompilerParams(vmem_limit_bytes=8 << 20),
    )(*placed)


def deliver_kernel(value_ref, out_ref):
    out_ref[0] = value_ref[...]


def delivered(value):
    return pl.pallas_call(
        deliver_kernel,
        name="deliver",
        out_shape=jax.ShapeDtypeStruct((1,) + value.shape, value.dtype),
        in_specs=[VMEM],
        out_specs=VMEM,
        compiler_params=pltpu.CompilerParams(vmem_limit_bytes=8 << 20),
    )(pltpu.with_memory_space_constraint(value, pltpu.VMEM))


def frequency_of(depth, lat, sections, size):
    upper = lat >= size // 2
    return (depth + upper * (sections // 2)) % sections


def home_of(row, size):
    half = size // 2
    return (row + 2) % half if row < half else row


def moved(value, inward=True):
    size = lax.axis_size("lat")
    route = [(row, home_of(row, size)) for row in range(size)]
    return lax.ppermute(value, "lat", route if inward else [(b, a) for a, b in route])


def swapped(rows):
    sections, size = (lax.axis_size("depth"), lax.axis_size("lat"))
    place = {}
    for row in range(size):
        lat = home_of(row, size)
        for depth in range(sections):
            place[frequency_of(depth, lat, sections, size), row] = depth * size + lat
    received = []
    for offset in (1, 0):
        route = []
        for member in range(sections):
            for row in range(offset, size - 1, 2):
                one, other = (place[member, row], place[member, row + 1])
                route += [(one, other), (other, one)]
        received.append(lax.ppermute(rows, ("depth", "lat"), route))
    return received


def exchanged(parts):
    return lax.all_to_all(parts, "depth", 0, 0)


def per_device(source_field, receiver_field, freq_index, slowness, ffd_coef, band, image_mask):
    sections = lax.axis_size("depth")
    lat, size = (lax.axis_index("lat"), lax.axis_size("lat"))
    member = frequency_of(lax.axis_index("depth"), lat, sections, size)
    height, width = slowness.shape[1:]
    levels = sections
    omega = 0.1 * (lax.dynamic_slice_in_dim(freq_index, member, 1).astype(F32) + 1.0)
    odd = lax.rem(lat, 2)
    weights_fore = jnp.where(odd == 1, *weights_of(4)[::-1])
    weights_back = jnp.where(odd == 1, *weights_of(2)[::-1])
    fields = []
    for field in (source_field, receiver_field):
        own = lax.dynamic_index_in_dim(field, member, 0, keepdims=False)
        fields.append(own.reshape(2 * height, width))

    wide, half, single = ((4 * height, width), (2 * height, width), (height, width))
    signed = jnp.where(image_mask[0] > 0, ffd_coef[0], -ffd_coef[0])
    own = moved(jnp.stack([slowness[0], signed]))
    fields = [moved(field) for field in fields]
    half_index = odd.astype(jnp.int32).reshape(1)
    share = BLOCK // 2
    pieces = lax.dynamic_slice_in_dim(band, odd * share, share, 2)
    pieces = exchanged(jnp.broadcast_to(pieces[None], (sections,) + pieces.shape))
    (params,) = call(copies_kernel, "copies", [((sections, 2) + single, F32)], 1000, own)
    pieces, _ = lax.optimization_barrier((pieces, params))
    params = exchanged(params)
    route = [(lat, lat + 1 - lat % 2 * 2) for lat in range(size)]
    other = lax.ppermute(pieces, "lat", route)
    (band,) = call(
        merge_kernel, "merge", [((2,) + pieces.shape, BF16)], 1000, half_index, pieces, other
    )
    rows, phased, angle = call(
        first_kernel, "first", [(wide, BF16), (wide, F32), (half, F32)], 1000, omega, params, *fields
    )
    stack = (sections, height, width)
    folded = (sections, 2 * height, width // 2)
    states, phases, angles = ([], [phased], [angle])
    products = []
    for level in range(levels):
        last = level == levels - 1
        first, second = swapped(rows)
        outs = [(wide, F32)] + ([] if last else [(half, F32)])
        lateral, *more = call(
            functools.partial(middle_kernel, level),
            "middle",
            outs,
            1 << 28,
            omega,
            params,
            band,
            weights_fore,
            rows,
        )
        angles += more
        outs = [(half, F32), (stack, F32)]
        outs += [] if last else [(wide, BF16), (wide, F32)]
        args = [params, weights_fore, lateral, first, second, phased] + more + products
        state, products, *more = call(
            functools.partial(step_kernel, level, last),
            "step",
            outs,
            1 << 20,
            *args,
            reuse={len(args) - 1: 1} if products else None,
        )
        products = [products]
        states.append(state)
        if not last:
            rows, phased = more
            phases.append(phased)

    image, images = call(
        image_kernel, "image", [(single, F32), (stack, F32)], 1000, exchanged(products[0])
    )
    images = exchanged(images)
    image = moved(image, False)

    level = levels - 1
    adjoint, scaled = call(
        functools.partial(adjoint_kernel, level),
        "adjoint",
        [(half, F32), (half, BF16)],
        1000,
        params,
        images,
        states[level],
    )
    terms = []
    for level in reversed(range(levels)):
        last = level == 0
        first, second = swapped(scaled)
        (lateral,) = call(
            middle_back_kernel, "middle_back", [(half, F32)], 1 << 28, band, weights_back, scaled
        )
        args = [omega, params, weights_back, lateral, first, second, adjoint, phases[level]]
        if last:
            args += terms
            outs = [(folded, BF16)]
        else:
            args += [angles[level], images, states[level - 1]]
            outs = [(folded[1:], BF16), (half, F32), (half, BF16)]
        term, *more = call(
            functools.partial(back_kernel, level, last),
            "back",
            outs,
            1 << 20,
            *args,
        )
        terms = [term] + terms
        if not last:
            adjoint, scaled = more
    (gradient,) = call(
        gradient_kernel, "gradient", [(single, F32)], 1000, exchanged(terms[0])
    )
    gradient = moved(gradient, False)
    return (delivered(image), delivered(gradient))


def solution(mesh):
    return jax.shard_map(
        per_device,
        mesh=mesh,
        in_specs=(
            P(None, None, "lat", None),
            P(None, None, "lat", None),
            P(),
            P("depth", "lat", None),
            P("depth", "lat", None),
            P("depth", None, None, None),
            P("depth", "lat", None),
        ),
        out_specs=(P("depth", "lat", None), P("depth", "lat", None)),
        check_vma=False,
    )
```

```python
import functools
import jax
import jax.numpy as jnp
import numpy as np
from jax import lax
from jax.experimental import pallas as pl
from jax.experimental.pallas import tpu as pltpu
from jax.sharding import PartitionSpec as P

HALO = 8
BLOCK = 128
PAIR = 2 * BLOCK
VMEM = pl.BlockSpec(memory_space=pltpu.VMEM)
SMEM = pl.BlockSpec(memory_space=pltpu.SMEM)
F32, BF16 = jnp.float32, jnp.bfloat16


def stencil_weight(distance):
    if distance == 0:
        return sum(-0.5 / k for k in range(1, HALO + 1))
    return 0.25 / abs(distance) if abs(distance) <= HALO else 0.0


def stencil_matrix(combos, shift):
    small = np.zeros((HALO, HALO))
    for row in range(HALO):
        for source in range(HALO):
            small[row, source] = stencil_weight(shift + source - row)
    return np.kron(np.eye(combos), small)


def split_weights(matrix):
    high = matrix.astype(jnp.bfloat16)
    low = (matrix - high.astype(np.float64)).astype(jnp.bfloat16)
    return np.concatenate([high, low], axis=0)


def weights_of(combos):
    own, after, before = [stencil_matrix(combos, shift) for shift in (0, HALO, -HALO)]
    even = np.concatenate([before, after, own], axis=1)
    odd = np.concatenate([after, before, own], axis=1)
    return [split_weights(matrix) for matrix in (even, odd)]


def cos_sin(theta):
    turns = jnp.floor(theta * 0.6366197723675814 + 0.5)
    rest = theta - turns * 1.5703125
    rest = rest - turns * 4.837512969970703e-4
    rest = rest - turns * 7.549789948768648e-8
    square = rest * rest
    sine = rest + rest * square * (
        -1.6666654611e-1 + square * (8.3321608736e-3 + square * -1.9515295891e-4)
    )
    cosine = (
        1.0
        - 0.5 * square
        + square
        * square
        * (4.166664568298827e-2 + square * (-1.388731625493765e-3 + square * 2.443315711809948e-5))
    )
    quadrant = turns.astype(jnp.int32)
    swap = (quadrant & 1) == 1
    sine_out = jnp.where(swap, cosine, sine)
    cosine_out = jnp.where(swap, sine, cosine)
    sine_out = jnp.where((quadrant & 2) == 2, -sine_out, sine_out)
    cosine_out = jnp.where(((quadrant + 1) & 2) == 2, -cosine_out, cosine_out)
    return (cosine_out, sine_out)


def dot(left, right):
    return jnp.dot(left, right, preferred_element_type=F32)


def dot_t(left, right):
    return lax.dot_general(left, right, (((1,), (1,)), ((), ())), preferred_element_type=F32)


def columns(chunk):
    return slice(chunk * PAIR, (chunk + 1) * PAIR)


def block_of(band_ref, index, offset):
    pair, place = (index // 2, index % 2)
    return jnp.concatenate([band_ref[half, pair, place, offset] for half in (0, 1)], axis=0)


def centre_of(band_ref, pair):
    first, second = (2 * pair, 2 * pair + 1)
    upper = [block_of(band_ref, first, 1), block_of(band_ref, second, 0)]
    lower = [block_of(band_ref, first, 2), block_of(band_ref, second, 1)]
    return jnp.concatenate(
        [jnp.concatenate(upper, axis=1), jnp.concatenate(lower, axis=1)], axis=0
    )


def edge_of(band_ref, pair, side):
    return block_of(band_ref, 2 * pair + side, 2 * side)


def share_kernel(half_ref, band_ref, out_ref, semaphores):
    share = out_ref.shape[3]
    rows = pl.ds(pl.multiple_of(half_ref[0] * share, share), share)
    copies = []
    for copy in range(out_ref.shape[0]):
        source = band_ref.at[:, :, rows, :]
        copies.append(pltpu.make_async_copy(source, out_ref.at[copy], semaphores.at[copy]))
        copies[-1].start()
    for copy in copies:
        copy.wait()


def merge_kernel(half_ref, own_ref, other_ref, out_ref):
    half = half_ref[0]
    out_ref[half] = own_ref[...]
    out_ref[1 - half] = other_ref[...]


def copies_kernel(value_ref, out_ref):
    for copy in range(out_ref.shape[0]):
        out_ref[copy] = value_ref[...]


def coef_of(params, level, cols):
    return jnp.abs(params[level, 1, :, cols])


def visible(params, level, cols, image):
    return jnp.where(params[level, 1, :, cols] > 0.0, image, 0.0)


def phase(fields, cosine, sine):
    parts = []
    for member in range(fields.shape[0] // (2 * HALO)):
        base = member * 2 * HALO
        real, imag = (fields[base : base + HALO], fields[base + HALO : base + 2 * HALO])
        parts.append(real * cosine - imag * sine)
        parts.append(real * sine + imag * cosine)
    return jnp.concatenate(parts, axis=0)


def first_kernel(omega_ref, params_ref, source_ref, receiver_ref, rows_ref, phased_ref):
    omega = omega_ref[0]
    for chunk in range(params_ref.shape[3] // PAIR):
        cols = columns(chunk)
        cosine, sine = cos_sin(omega * params_ref[0, 0, :, cols])
        fields = jnp.concatenate([source_ref[:, cols], receiver_ref[:, cols]], axis=0)
        phased = phase(fields.astype(F32), cosine, sine)
        phased_ref[:, cols] = phased
        rows_ref[:, cols] = phased.astype(BF16)


def middle_kernel(level, omega_ref, params_ref, band_ref, weights_ref, rows_ref, lateral_ref, *angle_refs):
    omega = omega_ref[0]
    pairs = band_ref.shape[1]
    height = rows_ref.shape[0]
    for pair in range(pairs):
        cols = columns(pair)
        rows = rows_ref[:, cols]
        total = dot(rows, centre_of(band_ref, pair))
        spread = dot(weights_ref[:, 2 * height : 3 * height], rows)
        total = total + (spread[:height] + spread[height:])
        zero = jnp.zeros((height, BLOCK), F32)
        left, right = (zero, zero)
        if pair > 0:
            before = rows_ref[:, pair * PAIR - BLOCK : pair * PAIR]
            left = dot(before, edge_of(band_ref, pair, 0))
        if pair < pairs - 1:
            after = rows_ref[:, (pair + 1) * PAIR : (pair + 1) * PAIR + BLOCK]
            right = dot(after, edge_of(band_ref, pair, 1))
        lateral_ref[:, cols] = total + jnp.concatenate([left, right], axis=1)
        if angle_refs:
            cosine, sine = cos_sin(omega * params_ref[level + 1, 0, :, cols])
            angle_refs[0][0:HALO, cols] = cosine
            angle_refs[0][HALO : 2 * HALO, cols] = sine


def sides(weights_ref, first_ref, second_ref, cols):
    both = jnp.concatenate([first_ref[:, cols], second_ref[:, cols]], axis=0)
    height = first_ref.shape[0]
    spread = dot(weights_ref[:, 0 : 2 * height], both)
    return spread[:height] + spread[height:]


def step_kernel(level, last, *refs):
    params, weights, lateral, first, second, phased = refs[:6]
    if last:
        state, products = refs[-2:]
    else:
        angle = refs[6]
        state, products, rows_next, phased_next = refs[-4:]
    halves = params.shape[3] // PAIR // 2
    for index in range(halves):
        for chunk in (index, index + halves):
            cols = columns(chunk)
            total = lateral[:, cols] + sides(weights, first, second, cols)
            coef = coef_of(params, level, cols)
            value = phased[:, cols]
            part = [slice(k * HALO, (k + 1) * HALO) for k in range(4)]
            source_re = value[part[0]] - coef * total[part[1]]
            source_im = value[part[1]] + coef * total[part[0]]
            receiver_re = value[part[2]] - coef * total[part[3]]
            receiver_im = value[part[3]] + coef * total[part[2]]
            state[0:HALO, cols] = source_re
            state[HALO : 2 * HALO, cols] = source_im
            product = source_re * receiver_re + source_im * receiver_im
            if not last:
                stepped = jnp.concatenate(
                    [source_re, source_im, receiver_re, receiver_im], axis=0
                )
                entering = stepped.astype(BF16).astype(F32)
                cosine, sine = (angle[0:HALO, cols], angle[HALO : 2 * HALO, cols])
                following = phase(entering, cosine, sine)
                phased_next[:, cols] = following
                rows_next[:, cols] = following.astype(BF16)
            products[level, :, cols] = product


def mean_of(parts_ref, cols):
    count = parts_ref.shape[0]
    total = parts_ref[0, :, cols].astype(F32)
    for member in range(1, count):
        total = total + parts_ref[member, :, cols].astype(F32)
    return total / count


def image_kernel(parts_ref, image_ref, copies_ref):
    for chunk in range(parts_ref.shape[2] // PAIR):
        cols = columns(chunk)
        image = mean_of(parts_ref, cols)
        image_ref[:, cols] = image
        for copy in range(copies_ref.shape[0]):
            copies_ref[copy, :, cols] = image


def gradient_kernel(parts_ref, gradient_ref):
    halves = parts_ref.shape[2] // PAIR
    for index in range(halves):
        gradient = mean_of(parts_ref, columns(index))
        gradient_ref[:, columns(index)] = gradient[:HALO]
        gradient_ref[:, columns(index + halves)] = gradient[HALO:]


def scaled_rows(adjoint, coef):
    return jnp.concatenate([adjoint[:HALO] * coef, adjoint[HALO:] * coef], axis=0).astype(BF16)


def weighted(masked, state):
    return jnp.concatenate([masked * state[:HALO], masked * state[HALO:]], axis=0)


def adjoint_kernel(level, params, images, state, adjoint, scaled):
    for chunk in range(images.shape[2] // PAIR):
        cols = columns(chunk)
        masked = visible(params, level, cols, images[level, :, cols])
        value = weighted(masked, state[:, cols])
        adjoint[:, cols] = value
        scaled[:, cols] = scaled_rows(value, coef_of(params, level, cols))


def middle_back_kernel(band_ref, weights_ref, rows_ref, lateral_ref):
    pairs = band_ref.shape[1]
    height = rows_ref.shape[0]
    for pair in range(pairs):
        cols = columns(pair)
        rows = rows_ref[:, cols]
        total = dot_t(rows, centre_of(band_ref, pair))
        spread = dot(weights_ref[:, 2 * height : 3 * height], rows)
        total = total + (spread[:height] + spread[height:])
        zero = jnp.zeros((height, BLOCK), F32)
        left, right = (zero, zero)
        if pair > 0:
            before = rows_ref[:, pair * PAIR - BLOCK : pair * PAIR]
            left = dot_t(before, edge_of(band_ref, pair - 1, 1))
        if pair < pairs - 1:
            after = rows_ref[:, (pair + 1) * PAIR : (pair + 1) * PAIR + BLOCK]
            right = dot_t(after, edge_of(band_ref, pair + 1, 0))
        lateral_ref[:, cols] = total + jnp.concatenate([left, right], axis=1)


def back_kernel(level, last, *refs):
    omega, params, weights, lateral, first, second, adjoint, phased = refs[:8]
    if last:
        term = refs[-1].at[0]
        for later, ref in enumerate(refs[8:-1]):
            refs[-1][later + 1] = ref[...]
    else:
        angle, images, state, term, adjoint_next, scaled_next = refs[8:]
    halves = term.shape[1] // PAIR
    for index in range(halves):
        pieces = []
        for chunk in (index, index + halves):
            cols = columns(chunk)
            total = lateral[:, cols] + sides(weights, first, second, cols)
            value = adjoint[:, cols]
            back_re = value[:HALO] + total[HALO:]
            back_im = value[HALO:] - total[:HALO]
            phase_re = phased[2 * HALO : 3 * HALO, cols]
            phase_im = phased[3 * HALO : 4 * HALO, cols]
            pieces.append(omega[0] * (back_im * phase_re - back_re * phase_im))
            if not last:
                cosine, sine = (angle[0:HALO, cols], angle[HALO : 2 * HALO, cols])
                upward = jnp.concatenate(
                    [back_re * cosine + back_im * sine, back_im * cosine - back_re * sine],
                    axis=0,
                )
                upward = upward.astype(BF16).astype(F32)
                masked = visible(params, level - 1, cols, images[level - 1, :, cols])
                following = weighted(masked, state[:, cols]) + upward
                adjoint_next[:, cols] = following
                scaled_next[:, cols] = scaled_rows(following, coef_of(params, level - 1, cols))
        term[:, columns(index)] = jnp.concatenate(pieces, axis=0).astype(BF16)


def call(kernel, name, outs, cost, *args, reuse=None):
    placed = []
    for arg in args:
        scalar = arg.shape == (1,)
        placed.append(arg if scalar else pltpu.with_memory_space_constraint(arg, pltpu.VMEM))
    return pl.pallas_call(
        kernel,
        name=name,
        out_shape=[pltpu.VMEM(shape, kind) for shape, kind in outs],
        in_specs=[SMEM if arg.shape == (1,) else VMEM for arg in args],
        out_specs=[VMEM] * len(outs),
        input_output_aliases=reuse or {},
        cost_estimate=pl.CostEstimate(flops=cost, bytes_accessed=1 << 20, transcendentals=0),
        compiler_params=pltpu.CompilerParams(vmem_limit_bytes=8 << 20),
    )(*placed)


def deliver_kernel(value_ref, out_ref):
    out_ref[0] = value_ref[...]


def delivered(value):
    return pl.pallas_call(
        deliver_kernel,
        name="deliver",
        out_shape=jax.ShapeDtypeStruct((1,) + value.shape, value.dtype),
        in_specs=[VMEM],
        out_specs=VMEM,
        compiler_params=pltpu.CompilerParams(vmem_limit_bytes=8 << 20),
    )(pltpu.with_memory_space_constraint(value, pltpu.VMEM))


def frequency_of(depth, lat, sections, size):
    upper = lat >= size // 2
    return (depth + upper * (sections // 2)) % sections


def home_of(row, size):
    half = size // 2
    return (row + 2) % half if row < half else row


def moved(value, inward=True):
    size = lax.axis_size("lat")
    route = [(row, home_of(row, size)) for row in range(size)]
    return lax.ppermute(value, "lat", route if inward else [(b, a) for a, b in route])


def swapped(rows):
    sections, size = (lax.axis_size("depth"), lax.axis_size("lat"))
    place = {}
    for row in range(size):
        lat = home_of(row, size)
        for depth in range(sections):
            place[frequency_of(depth, lat, sections, size), row] = depth * size + lat
    received = []
    for offset in (1, 0):
        route = []
        for member in range(sections):
            for row in range(offset, size - 1, 2):
                one, other = (place[member, row], place[member, row + 1])
                route += [(one, other), (other, one)]
        received.append(lax.ppermute(rows, ("depth", "lat"), route))
    return received


def exchanged(parts):
    return lax.all_to_all(parts, "depth", 0, 0)


def per_device(source_field, receiver_field, freq_index, slowness, ffd_coef, band, image_mask):
    sections = lax.axis_size("depth")
    lat, size = (lax.axis_index("lat"), lax.axis_size("lat"))
    member = frequency_of(lax.axis_index("depth"), lat, sections, size)
    height, width = slowness.shape[1:]
    levels = sections
    omega = 0.1 * (lax.dynamic_slice_in_dim(freq_index, member, 1).astype(F32) + 1.0)
    odd = lax.rem(lat, 2)
    weights_fore = jnp.where(odd == 1, *weights_of(4)[::-1])
    weights_back = jnp.where(odd == 1, *weights_of(2)[::-1])
    fields = []
    for field in (source_field, receiver_field):
        own = lax.dynamic_index_in_dim(field, member, 0, keepdims=False)
        fields.append(own.reshape(2 * height, width))

    wide, half, single = ((4 * height, width), (2 * height, width), (height, width))
    signed = jnp.where(image_mask[0] > 0, ffd_coef[0], -ffd_coef[0])
    own = moved(jnp.stack([slowness[0], signed]))
    fields = [moved(field) for field in fields]
    half_index = odd.astype(jnp.int32).reshape(1)
    share = BLOCK // 2
    pieces = pl.pallas_call(
        share_kernel,
        name="share",
        out_shape=jax.ShapeDtypeStruct((sections,) + band.shape[:2] + (share, BLOCK), BF16),
        in_specs=[SMEM, pl.BlockSpec(memory_space=pl.ANY)],
        out_specs=pl.BlockSpec(memory_space=pl.ANY),
        scratch_shapes=[pltpu.SemaphoreType.DMA((sections,))],
        compiler_params=pltpu.CompilerParams(vmem_limit_bytes=8 << 20),
    )(half_index, pltpu.with_memory_space_constraint(band, pltpu.VMEM))
    pieces = exchanged(pieces)
    (params,) = call(copies_kernel, "copies", [((sections, 2) + single, F32)], 1000, own)
    pieces, _ = lax.optimization_barrier((pieces, params))
    params = exchanged(params)
    route = [(lat, lat + 1 - lat % 2 * 2) for lat in range(size)]
    other = lax.ppermute(pieces, "lat", route)
    (band,) = call(
        merge_kernel, "merge", [((2,) + pieces.shape, BF16)], 1000, half_index, pieces, other
    )
    rows, phased = call(
        first_kernel, "first", [(wide, BF16), (wide, F32)], 1000, omega, params, *fields
    )
    stack = (sections, height, width)
    folded = (sections, 2 * height, width // 2)
    states, phases, angles = ([], [phased], [None])
    products = []
    for level in range(levels):
        last = level == levels - 1
        first, second = swapped(rows)
        outs = [(wide, F32)] + ([] if last else [(half, F32)])
        lateral, *more = call(
            functools.partial(middle_kernel, level),
            "middle",
            outs,
            1 << 28,
            omega,
            params,
            band,
            weights_fore,
            rows,
        )
        angles += more
        outs = [(half, F32), (stack, F32)]
        outs += [] if last else [(wide, BF16), (wide, F32)]
        args = [params, weights_fore, lateral, first, second, phased] + more + products
        state, products, *more = call(
            functools.partial(step_kernel, level, last),
            "step",
            outs,
            1 << 20,
            *args,
            reuse={len(args) - 1: 1} if products else None,
        )
        products = [products]
        states.append(state)
        if not last:
            rows, phased = more
            phases.append(phased)

    image, images = call(
        image_kernel, "image", [(single, F32), (stack, F32)], 1000, exchanged(products[0])
    )
    images = exchanged(images)
    image = moved(image, False)

    level = levels - 1
    adjoint, scaled = call(
        functools.partial(adjoint_kernel, level),
        "adjoint",
        [(half, F32), (half, BF16)],
        1000,
        params,
        images,
        states[level],
    )
    terms = []
    for level in reversed(range(levels)):
        last = level == 0
        first, second = swapped(scaled)
        (lateral,) = call(
            middle_back_kernel, "middle_back", [(half, F32)], 1 << 28, band, weights_back, scaled
        )
        args = [omega, params, weights_back, lateral, first, second, adjoint, phases[level]]
        if last:
            args += terms
            outs = [(folded, BF16)]
        else:
            args += [angles[level], images, states[level - 1]]
            outs = [(folded[1:], BF16), (half, F32), (half, BF16)]
        term, *more = call(
            functools.partial(back_kernel, level, last),
            "back",
            outs,
            1 << 20,
            *args,
        )
        terms = [term] + terms
        if not last:
            adjoint, scaled = more
    (gradient,) = call(
        gradient_kernel, "gradient", [(single, F32)], 1000, exchanged(terms[0])
    )
    gradient = moved(gradient, False)
    return (delivered(image), delivered(gradient))


def solution(mesh):
    return jax.shard_map(
        per_device,
        mesh=mesh,
        in_specs=(
            P(None, None, "lat", None),
            P(None, None, "lat", None),
            P(),
            P("depth", "lat", None),
            P("depth", "lat", None),
            P("depth", None, None, None),
            P("depth", "lat", None),
        ),
        out_specs=(P("depth", "lat", None), P("depth", "lat", None)),
        check_vma=False,
    )
```

```python
import functools
import jax
import jax.numpy as jnp
import numpy as np
from jax import lax
from jax.experimental import pallas as pl
from jax.experimental.pallas import tpu as pltpu
from jax.sharding import PartitionSpec as P

HALO = 8
BLOCK = 128
PAIR = 2 * BLOCK
VMEM = pl.BlockSpec(memory_space=pltpu.VMEM)
SMEM = pl.BlockSpec(memory_space=pltpu.SMEM)
F32, BF16 = jnp.float32, jnp.bfloat16


def stencil_weight(distance):
    if distance == 0:
        return sum(-0.5 / k for k in range(1, HALO + 1))
    return 0.25 / abs(distance) if abs(distance) <= HALO else 0.0


def stencil_matrix(combos, shift):
    small = np.zeros((HALO, HALO))
    for row in range(HALO):
        for source in range(HALO):
            small[row, source] = stencil_weight(shift + source - row)
    return np.kron(np.eye(combos), small)


def split_weights(matrix):
    high = matrix.astype(jnp.bfloat16)
    low = (matrix - high.astype(np.float64)).astype(jnp.bfloat16)
    return np.concatenate([high, low], axis=0)


def weights_of(combos):
    own, after, before = [stencil_matrix(combos, shift) for shift in (0, HALO, -HALO)]
    even = np.concatenate([before, after, own], axis=1)
    odd = np.concatenate([after, before, own], axis=1)
    return [split_weights(matrix) for matrix in (even, odd)]


def cos_sin(theta):
    turns = jnp.floor(theta * 0.6366197723675814 + 0.5)
    rest = theta - turns * 1.5703125
    rest = rest - turns * 4.837512969970703e-4
    rest = rest - turns * 7.549789948768648e-8
    square = rest * rest
    sine = rest + rest * square * (
        -1.6666654611e-1 + square * (8.3321608736e-3 + square * -1.9515295891e-4)
    )
    cosine = (
        1.0
        - 0.5 * square
        + square
        * square
        * (4.166664568298827e-2 + square * (-1.388731625493765e-3 + square * 2.443315711809948e-5))
    )
    quadrant = turns.astype(jnp.int32)
    swap = (quadrant & 1) == 1
    sine_out = jnp.where(swap, cosine, sine)
    cosine_out = jnp.where(swap, sine, cosine)
    sine_out = jnp.where((quadrant & 2) == 2, -sine_out, sine_out)
    cosine_out = jnp.where(((quadrant + 1) & 2) == 2, -cosine_out, cosine_out)
    return (cosine_out, sine_out)


def dot(left, right):
    return jnp.dot(left, right, preferred_element_type=F32)


def dot_t(left, right):
    return lax.dot_general(left, right, (((1,), (1,)), ((), ())), preferred_element_type=F32)


def columns(chunk):
    return slice(chunk * PAIR, (chunk + 1) * PAIR)


def block_of(band_ref, index, offset):
    pair, place = (index // 2, index % 2)
    return jnp.concatenate([band_ref[half, pair, place, offset] for half in (0, 1)], axis=0)


def centre_of(band_ref, pair):
    first, second = (2 * pair, 2 * pair + 1)
    upper = [block_of(band_ref, first, 1), block_of(band_ref, second, 0)]
    lower = [block_of(band_ref, first, 2), block_of(band_ref, second, 1)]
    return jnp.concatenate(
        [jnp.concatenate(upper, axis=1), jnp.concatenate(lower, axis=1)], axis=0
    )


def edge_of(band_ref, pair, side):
    return block_of(band_ref, 2 * pair + side, 2 * side)


def share_kernel(half_ref, band_ref, out_ref, semaphores):
    share = out_ref.shape[3]
    rows = pl.ds(pl.multiple_of(half_ref[0] * share, share), share)
    copies = []
    for copy in range(out_ref.shape[0]):
        source = band_ref.at[:, :, rows, :]
        copies.append(pltpu.make_async_copy(source, out_ref.at[copy], semaphores.at[copy]))
        copies[-1].start()
    for copy in copies:
        copy.wait()


def merge_kernel(half_ref, own_ref, other_ref, out_ref):
    half = half_ref[0]
    out_ref[half] = own_ref[...]
    out_ref[1 - half] = other_ref[...]


def copies_kernel(value_ref, out_ref):
    for copy in range(out_ref.shape[0]):
        out_ref[copy] = value_ref[...]


def coef_of(params, level, cols):
    return jnp.abs(params[level, 1, :, cols])


def visible(params, level, cols, image):
    return jnp.where(params[level, 1, :, cols] > 0.0, image, 0.0)


def phase(fields, cosine, sine):
    parts = []
    for member in range(fields.shape[0] // (2 * HALO)):
        base = member * 2 * HALO
        real, imag = (fields[base : base + HALO], fields[base + HALO : base + 2 * HALO])
        parts.append(real * cosine - imag * sine)
        parts.append(real * sine + imag * cosine)
    return jnp.concatenate(parts, axis=0)


def first_kernel(omega_ref, params_ref, source_ref, receiver_ref, rows_ref, phased_ref):
    omega = omega_ref[0]
    for chunk in range(params_ref.shape[3] // PAIR):
        cols = columns(chunk)
        cosine, sine = cos_sin(omega * params_ref[0, 0, :, cols])
        fields = jnp.concatenate([source_ref[:, cols], receiver_ref[:, cols]], axis=0)
        phased = phase(fields.astype(F32), cosine, sine)
        phased_ref[:, cols] = phased
        rows_ref[:, cols] = phased.astype(BF16)


def middle_kernel(level, omega_ref, params_ref, band_ref, weights_ref, rows_ref, lateral_ref, *angle_refs):
    omega = omega_ref[0]
    pairs = band_ref.shape[1]
    height = rows_ref.shape[0]
    for pair in range(pairs):
        cols = columns(pair)
        rows = rows_ref[:, cols]
        total = dot(rows, centre_of(band_ref, pair))
        spread = dot(weights_ref[:, 2 * height : 3 * height], rows)
        total = total + (spread[:height] + spread[height:])
        zero = jnp.zeros((height, BLOCK), F32)
        left, right = (zero, zero)
        if pair > 0:
            before = rows_ref[:, pair * PAIR - BLOCK : pair * PAIR]
            left = dot(before, edge_of(band_ref, pair, 0))
        if pair < pairs - 1:
            after = rows_ref[:, (pair + 1) * PAIR : (pair + 1) * PAIR + BLOCK]
            right = dot(after, edge_of(band_ref, pair, 1))
        lateral_ref[:, cols] = total + jnp.concatenate([left, right], axis=1)
        if angle_refs:
            cosine, sine = cos_sin(omega * params_ref[level + 1, 0, :, cols])
            angle_refs[0][0:HALO, cols] = cosine
            angle_refs[0][HALO : 2 * HALO, cols] = sine


def sides(weights_ref, first_ref, second_ref, cols):
    both = jnp.concatenate([first_ref[:, cols], second_ref[:, cols]], axis=0)
    height = first_ref.shape[0]
    spread = dot(weights_ref[:, 0 : 2 * height], both)
    return spread[:height] + spread[height:]


def step_kernel(level, last, *refs):
    params, weights, lateral, first, second, phased = refs[:6]
    if last:
        state, products = refs[-2:]
    else:
        angle = refs[6]
        state, products, rows_next, phased_next = refs[-4:]
    halves = params.shape[3] // PAIR // 2
    for index in range(halves):
        for chunk in (index, index + halves):
            cols = columns(chunk)
            total = lateral[:, cols] + sides(weights, first, second, cols)
            coef = coef_of(params, level, cols)
            value = phased[:, cols]
            part = [slice(k * HALO, (k + 1) * HALO) for k in range(4)]
            source_re = value[part[0]] - coef * total[part[1]]
            source_im = value[part[1]] + coef * total[part[0]]
            receiver_re = value[part[2]] - coef * total[part[3]]
            receiver_im = value[part[3]] + coef * total[part[2]]
            state[0:HALO, cols] = source_re
            state[HALO : 2 * HALO, cols] = source_im
            product = source_re * receiver_re + source_im * receiver_im
            if not last:
                stepped = jnp.concatenate(
                    [source_re, source_im, receiver_re, receiver_im], axis=0
                )
                entering = stepped.astype(BF16).astype(F32)
                cosine, sine = (angle[0:HALO, cols], angle[HALO : 2 * HALO, cols])
                following = phase(entering, cosine, sine)
                phased_next[:, cols] = following
                rows_next[:, cols] = following.astype(BF16)
            products[level, :, cols] = product


def mean_of(parts_ref, cols):
    count = parts_ref.shape[0]
    total = parts_ref[0, :, cols].astype(F32)
    for member in range(1, count):
        total = total + parts_ref[member, :, cols].astype(F32)
    return total / count


def image_kernel(parts_ref, image_ref, copies_ref):
    for chunk in range(parts_ref.shape[2] // PAIR):
        cols = columns(chunk)
        image = mean_of(parts_ref, cols)
        image_ref[:, cols] = image
        for copy in range(copies_ref.shape[0]):
            copies_ref[copy, :, cols] = image


def gradient_kernel(parts_ref, image_ref, both_ref):
    both_ref[0] = image_ref[...]
    halves = parts_ref.shape[2] // PAIR
    for index in range(halves):
        gradient = mean_of(parts_ref, columns(index))
        both_ref[1, :, columns(index)] = gradient[:HALO]
        both_ref[1, :, columns(index + halves)] = gradient[HALO:]


def scaled_rows(adjoint, coef):
    return jnp.concatenate([adjoint[:HALO] * coef, adjoint[HALO:] * coef], axis=0).astype(BF16)


def weighted(masked, state):
    return jnp.concatenate([masked * state[:HALO], masked * state[HALO:]], axis=0)


def adjoint_kernel(level, params, images, state, adjoint, scaled):
    for chunk in range(images.shape[2] // PAIR):
        cols = columns(chunk)
        masked = visible(params, level, cols, images[level, :, cols])
        value = weighted(masked, state[:, cols])
        adjoint[:, cols] = value
        scaled[:, cols] = scaled_rows(value, coef_of(params, level, cols))


def middle_back_kernel(band_ref, weights_ref, rows_ref, lateral_ref):
    pairs = band_ref.shape[1]
    height = rows_ref.shape[0]
    for pair in range(pairs):
        cols = columns(pair)
        rows = rows_ref[:, cols]
        total = dot_t(rows, centre_of(band_ref, pair))
        spread = dot(weights_ref[:, 2 * height : 3 * height], rows)
        total = total + (spread[:height] + spread[height:])
        zero = jnp.zeros((height, BLOCK), F32)
        left, right = (zero, zero)
        if pair > 0:
            before = rows_ref[:, pair * PAIR - BLOCK : pair * PAIR]
            left = dot_t(before, edge_of(band_ref, pair - 1, 1))
        if pair < pairs - 1:
            after = rows_ref[:, (pair + 1) * PAIR : (pair + 1) * PAIR + BLOCK]
            right = dot_t(after, edge_of(band_ref, pair + 1, 0))
        lateral_ref[:, cols] = total + jnp.concatenate([left, right], axis=1)


def back_kernel(level, last, *refs):
    omega, params, weights, lateral, first, second, adjoint, phased = refs[:8]
    if last:
        term = refs[-1].at[0]
        for later, ref in enumerate(refs[8:-1]):
            refs[-1][later + 1] = ref[...]
    else:
        angle, images, state, term, adjoint_next, scaled_next = refs[8:]
    halves = term.shape[1] // PAIR
    for index in range(halves):
        pieces = []
        for chunk in (index, index + halves):
            cols = columns(chunk)
            total = lateral[:, cols] + sides(weights, first, second, cols)
            value = adjoint[:, cols]
            back_re = value[:HALO] + total[HALO:]
            back_im = value[HALO:] - total[:HALO]
            phase_re = phased[2 * HALO : 3 * HALO, cols]
            phase_im = phased[3 * HALO : 4 * HALO, cols]
            pieces.append(omega[0] * (back_im * phase_re - back_re * phase_im))
            if not last:
                cosine, sine = (angle[0:HALO, cols], angle[HALO : 2 * HALO, cols])
                upward = jnp.concatenate(
                    [back_re * cosine + back_im * sine, back_im * cosine - back_re * sine],
                    axis=0,
                )
                upward = upward.astype(BF16).astype(F32)
                masked = visible(params, level - 1, cols, images[level - 1, :, cols])
                following = weighted(masked, state[:, cols]) + upward
                adjoint_next[:, cols] = following
                scaled_next[:, cols] = scaled_rows(following, coef_of(params, level - 1, cols))
        term[:, columns(index)] = jnp.concatenate(pieces, axis=0).astype(BF16)


def call(kernel, name, outs, cost, *args, reuse=None):
    placed = []
    for arg in args:
        scalar = arg.shape == (1,)
        placed.append(arg if scalar else pltpu.with_memory_space_constraint(arg, pltpu.VMEM))
    return pl.pallas_call(
        kernel,
        name=name,
        out_shape=[pltpu.VMEM(shape, kind) for shape, kind in outs],
        in_specs=[SMEM if arg.shape == (1,) else VMEM for arg in args],
        out_specs=[VMEM] * len(outs),
        input_output_aliases=reuse or {},
        cost_estimate=pl.CostEstimate(flops=cost, bytes_accessed=1 << 20, transcendentals=0),
        compiler_params=pltpu.CompilerParams(vmem_limit_bytes=8 << 20),
    )(*placed)


def deliver_kernel(both_ref, image_ref, gradient_ref):
    image_ref[0] = both_ref[0]
    gradient_ref[0] = both_ref[1]


def delivered(both):
    out = jax.ShapeDtypeStruct((1,) + both.shape[1:], both.dtype)
    return pl.pallas_call(
        deliver_kernel,
        name="deliver",
        out_shape=(out, out),
        in_specs=[VMEM],
        out_specs=(VMEM, VMEM),
        compiler_params=pltpu.CompilerParams(vmem_limit_bytes=8 << 20),
    )(pltpu.with_memory_space_constraint(both, pltpu.VMEM))


def frequency_of(depth, lat, sections, size):
    upper = lat >= size // 2
    return (depth + upper * (sections // 2)) % sections


def home_of(row, size):
    half = size // 2
    return (row + 2) % half if row < half else row


def moved(value, inward=True):
    size = lax.axis_size("lat")
    route = [(row, home_of(row, size)) for row in range(size)]
    return lax.ppermute(value, "lat", route if inward else [(b, a) for a, b in route])


def swapped(rows):
    sections, size = (lax.axis_size("depth"), lax.axis_size("lat"))
    place = {}
    for row in range(size):
        lat = home_of(row, size)
        for depth in range(sections):
            place[frequency_of(depth, lat, sections, size), row] = depth * size + lat
    received = []
    for offset in (1, 0):
        route = []
        for member in range(sections):
            for row in range(offset, size - 1, 2):
                one, other = (place[member, row], place[member, row + 1])
                route += [(one, other), (other, one)]
        received.append(lax.ppermute(rows, ("depth", "lat"), route))
    return received


def exchanged(parts):
    return lax.all_to_all(parts, "depth", 0, 0)


def per_device(source_field, receiver_field, freq_index, slowness, ffd_coef, band, image_mask):
    sections = lax.axis_size("depth")
    lat, size = (lax.axis_index("lat"), lax.axis_size("lat"))
    member = frequency_of(lax.axis_index("depth"), lat, sections, size)
    height, width = slowness.shape[1:]
    levels = sections
    omega = 0.1 * (lax.dynamic_slice_in_dim(freq_index, member, 1).astype(F32) + 1.0)
    odd = lax.rem(lat, 2)
    weights_fore = jnp.where(odd == 1, *weights_of(4)[::-1])
    weights_back = jnp.where(odd == 1, *weights_of(2)[::-1])
    fields = []
    for field in (source_field, receiver_field):
        own = lax.dynamic_index_in_dim(field, member, 0, keepdims=False)
        fields.append(own.reshape(2 * height, width))

    wide, half, single = ((4 * height, width), (2 * height, width), (height, width))
    signed = jnp.where(image_mask[0] > 0, ffd_coef[0], -ffd_coef[0])
    own = moved(jnp.stack([slowness[0], signed]))
    fields = [moved(field) for field in fields]
    half_index = odd.astype(jnp.int32).reshape(1)
    share = BLOCK // 2
    pieces = pl.pallas_call(
        share_kernel,
        name="share",
        out_shape=jax.ShapeDtypeStruct((sections,) + band.shape[:2] + (share, BLOCK), BF16),
        in_specs=[SMEM, pl.BlockSpec(memory_space=pl.ANY)],
        out_specs=pl.BlockSpec(memory_space=pl.ANY),
        scratch_shapes=[pltpu.SemaphoreType.DMA((sections,))],
        compiler_params=pltpu.CompilerParams(vmem_limit_bytes=8 << 20),
    )(half_index, pltpu.with_memory_space_constraint(band, pltpu.VMEM))
    pieces = exchanged(pieces)
    (params,) = call(copies_kernel, "copies", [((sections, 2) + single, F32)], 1000, own)
    pieces, _ = lax.optimization_barrier((pieces, params))
    params = exchanged(params)
    route = [(lat, lat + 1 - lat % 2 * 2) for lat in range(size)]
    other = lax.ppermute(pieces, "lat", route)
    (band,) = call(
        merge_kernel, "merge", [((2,) + pieces.shape, BF16)], 1000, half_index, pieces, other
    )
    rows, phased = call(
        first_kernel, "first", [(wide, BF16), (wide, F32)], 1000, omega, params, *fields
    )
    stack = (sections, height, width)
    folded = (sections, 2 * height, width // 2)
    states, phases, angles = ([], [phased], [None])
    products = []
    for level in range(levels):
        last = level == levels - 1
        first, second = swapped(rows)
        outs = [(wide, F32)] + ([] if last else [(half, F32)])
        lateral, *more = call(
            functools.partial(middle_kernel, level),
            "middle",
            outs,
            1 << 28,
            omega,
            params,
            band,
            weights_fore,
            rows,
        )
        angles += more
        outs = [(half, F32), (stack, F32)]
        outs += [] if last else [(wide, BF16), (wide, F32)]
        args = [params, weights_fore, lateral, first, second, phased] + more + products
        state, products, *more = call(
            functools.partial(step_kernel, level, last),
            "step",
            outs,
            1 << 20,
            *args,
            reuse={len(args) - 1: 1} if products else None,
        )
        products = [products]
        states.append(state)
        if not last:
            rows, phased = more
            phases.append(phased)

    image, images = call(
        image_kernel, "image", [(single, F32), (stack, F32)], 1000, exchanged(products[0])
    )
    images = exchanged(images)

    level = levels - 1
    adjoint, scaled = call(
        functools.partial(adjoint_kernel, level),
        "adjoint",
        [(half, F32), (half, BF16)],
        1000,
        params,
        images,
        states[level],
    )
    terms = []
    for level in reversed(range(levels)):
        last = level == 0
        first, second = swapped(scaled)
        (lateral,) = call(
            middle_back_kernel, "middle_back", [(half, F32)], 1 << 28, band, weights_back, scaled
        )
        args = [omega, params, weights_back, lateral, first, second, adjoint, phases[level]]
        if last:
            args += terms
            outs = [(folded, BF16)]
        else:
            args += [angles[level], images, states[level - 1]]
            outs = [(folded[1:], BF16), (half, F32), (half, BF16)]
        term, *more = call(
            functools.partial(back_kernel, level, last),
            "back",
            outs,
            1 << 20,
            *args,
        )
        terms = [term] + terms
        if not last:
            adjoint, scaled = more
    (both,) = call(
        gradient_kernel, "gradient", [((2,) + single, F32)], 1000, exchanged(terms[0]), image
    )
    return delivered(moved(both, False))


def solution(mesh):
    return jax.shard_map(
        per_device,
        mesh=mesh,
        in_specs=(
            P(None, None, "lat", None),
            P(None, None, "lat", None),
            P(),
            P("depth", "lat", None),
            P("depth", "lat", None),
            P("depth", None, None, None),
            P("depth", "lat", None),
        ),
        out_specs=(P("depth", "lat", None), P("depth", "lat", None)),
        check_vma=False,
    )
```

```python
import functools
import jax
import jax.numpy as jnp
import numpy as np
from jax import lax
from jax.experimental import pallas as pl
from jax.experimental.pallas import tpu as pltpu
from jax.sharding import PartitionSpec as P

HALO = 8
BLOCK = 128
PAIR = 2 * BLOCK
VMEM = pl.BlockSpec(memory_space=pltpu.VMEM)
SMEM = pl.BlockSpec(memory_space=pltpu.SMEM)
F32, BF16 = jnp.float32, jnp.bfloat16


def stencil_weight(distance):
    if distance == 0:
        return sum(-0.5 / k for k in range(1, HALO + 1))
    return 0.25 / abs(distance) if abs(distance) <= HALO else 0.0


def stencil_matrix(combos, shift):
    small = np.zeros((HALO, HALO))
    for row in range(HALO):
        for source in range(HALO):
            small[row, source] = stencil_weight(shift + source - row)
    return np.kron(np.eye(combos), small)


def split_weights(matrix):
    high = matrix.astype(jnp.bfloat16)
    low = (matrix - high.astype(np.float64)).astype(jnp.bfloat16)
    return np.concatenate([high, low], axis=0)


def weights_of(combos):
    own, after, before = [stencil_matrix(combos, shift) for shift in (0, HALO, -HALO)]
    even = np.concatenate([before, after, own], axis=1)
    odd = np.concatenate([after, before, own], axis=1)
    return [split_weights(matrix) for matrix in (even, odd)]


def cos_sin(theta):
    turns = jnp.floor(theta * 0.6366197723675814 + 0.5)
    rest = theta - turns * 1.5703125
    rest = rest - turns * 4.837512969970703e-4
    rest = rest - turns * 7.549789948768648e-8
    square = rest * rest
    sine = rest + rest * square * (
        -1.6666654611e-1 + square * (8.3321608736e-3 + square * -1.9515295891e-4)
    )
    cosine = (
        1.0
        - 0.5 * square
        + square
        * square
        * (4.166664568298827e-2 + square * (-1.388731625493765e-3 + square * 2.443315711809948e-5))
    )
    quadrant = turns.astype(jnp.int32)
    swap = (quadrant & 1) == 1
    sine_out = jnp.where(swap, cosine, sine)
    cosine_out = jnp.where(swap, sine, cosine)
    sine_out = jnp.where((quadrant & 2) == 2, -sine_out, sine_out)
    cosine_out = jnp.where(((quadrant + 1) & 2) == 2, -cosine_out, cosine_out)
    return (cosine_out, sine_out)


def dot(left, right):
    return jnp.dot(left, right, preferred_element_type=F32)


def dot_t(left, right):
    return lax.dot_general(left, right, (((1,), (1,)), ((), ())), preferred_element_type=F32)


def columns(chunk):
    return slice(chunk * PAIR, (chunk + 1) * PAIR)


def block_of(band_ref, index, offset):
    pair, place = (index // 2, index % 2)
    return jnp.concatenate([band_ref[half, pair, place, offset] for half in (0, 1)], axis=0)


def centre_of(band_ref, pair):
    first, second = (2 * pair, 2 * pair + 1)
    upper = [block_of(band_ref, first, 1), block_of(band_ref, second, 0)]
    lower = [block_of(band_ref, first, 2), block_of(band_ref, second, 1)]
    return jnp.concatenate(
        [jnp.concatenate(upper, axis=1), jnp.concatenate(lower, axis=1)], axis=0
    )


def edge_of(band_ref, pair, side):
    return block_of(band_ref, 2 * pair + side, 2 * side)


def share_kernel(half_ref, band_ref, out_ref, semaphores):
    share = out_ref.shape[3]
    rows = pl.ds(pl.multiple_of(half_ref[0] * share, share), share)
    copies = []
    for copy in range(out_ref.shape[0]):
        source = band_ref.at[:, :, rows, :]
        copies.append(pltpu.make_async_copy(source, out_ref.at[copy], semaphores.at[copy]))
        copies[-1].start()
    for copy in copies:
        copy.wait()


def merge_kernel(half_ref, own_ref, other_ref, out_ref):
    half = half_ref[0]
    out_ref[half] = own_ref[...]
    out_ref[1 - half] = other_ref[...]


def copies_kernel(value_ref, out_ref, semaphores):
    copies = []
    for copy in range(out_ref.shape[0]):
        copies.append(pltpu.make_async_copy(value_ref, out_ref.at[copy], semaphores.at[copy]))
        copies[-1].start()
    for copy in copies:
        copy.wait()


def coef_of(params, level, cols):
    return jnp.abs(params[level, 1, :, cols])


def visible(params, level, cols, image):
    return jnp.where(params[level, 1, :, cols] > 0.0, image, 0.0)


def phase(fields, cosine, sine):
    parts = []
    for member in range(fields.shape[0] // (2 * HALO)):
        base = member * 2 * HALO
        real, imag = (fields[base : base + HALO], fields[base + HALO : base + 2 * HALO])
        parts.append(real * cosine - imag * sine)
        parts.append(real * sine + imag * cosine)
    return jnp.concatenate(parts, axis=0)


def first_kernel(omega_ref, params_ref, source_ref, receiver_ref, rows_ref, phased_ref):
    omega = omega_ref[0]
    for chunk in range(params_ref.shape[3] // PAIR):
        cols = columns(chunk)
        cosine, sine = cos_sin(omega * params_ref[0, 0, :, cols])
        fields = jnp.concatenate([source_ref[:, cols], receiver_ref[:, cols]], axis=0)
        phased = phase(fields.astype(F32), cosine, sine)
        phased_ref[:, cols] = phased
        rows_ref[:, cols] = phased.astype(BF16)


def middle_kernel(level, omega_ref, params_ref, band_ref, weights_ref, rows_ref, lateral_ref, *angle_refs):
    omega = omega_ref[0]
    pairs = band_ref.shape[1]
    height = rows_ref.shape[0]
    for pair in range(pairs):
        cols = columns(pair)
        rows = rows_ref[:, cols]
        total = dot(rows, centre_of(band_ref, pair))
        spread = dot(weights_ref[:, 2 * height : 3 * height], rows)
        total = total + (spread[:height] + spread[height:])
        zero = jnp.zeros((height, BLOCK), F32)
        left, right = (zero, zero)
        if pair > 0:
            before = rows_ref[:, pair * PAIR - BLOCK : pair * PAIR]
            left = dot(before, edge_of(band_ref, pair, 0))
        if pair < pairs - 1:
            after = rows_ref[:, (pair + 1) * PAIR : (pair + 1) * PAIR + BLOCK]
            right = dot(after, edge_of(band_ref, pair, 1))
        lateral_ref[:, cols] = total + jnp.concatenate([left, right], axis=1)
        if angle_refs:
            cosine, sine = cos_sin(omega * params_ref[level + 1, 0, :, cols])
            angle_refs[0][0:HALO, cols] = cosine
            angle_refs[0][HALO : 2 * HALO, cols] = sine


def sides(weights_ref, first_ref, second_ref, cols):
    both = jnp.concatenate([first_ref[:, cols], second_ref[:, cols]], axis=0)
    height = first_ref.shape[0]
    spread = dot(weights_ref[:, 0 : 2 * height], both)
    return spread[:height] + spread[height:]


def step_kernel(level, last, *refs):
    params, weights, lateral, first, second, phased = refs[:6]
    if last:
        state, products = refs[-2:]
    else:
        angle = refs[6]
        state, products, rows_next, phased_next = refs[-4:]
    halves = params.shape[3] // PAIR // 2
    for index in range(halves):
        for chunk in (index, index + halves):
            cols = columns(chunk)
            total = lateral[:, cols] + sides(weights, first, second, cols)
            coef = coef_of(params, level, cols)
            value = phased[:, cols]
            part = [slice(k * HALO, (k + 1) * HALO) for k in range(4)]
            source_re = value[part[0]] - coef * total[part[1]]
            source_im = value[part[1]] + coef * total[part[0]]
            receiver_re = value[part[2]] - coef * total[part[3]]
            receiver_im = value[part[3]] + coef * total[part[2]]
            state[0:HALO, cols] = source_re
            state[HALO : 2 * HALO, cols] = source_im
            product = source_re * receiver_re + source_im * receiver_im
            if not last:
                stepped = jnp.concatenate(
                    [source_re, source_im, receiver_re, receiver_im], axis=0
                )
                entering = stepped.astype(BF16).astype(F32)
                cosine, sine = (angle[0:HALO, cols], angle[HALO : 2 * HALO, cols])
                following = phase(entering, cosine, sine)
                phased_next[:, cols] = following
                rows_next[:, cols] = following.astype(BF16)
            products[level, :, cols] = product


def mean_of(parts_ref, cols):
    count = parts_ref.shape[0]
    total = parts_ref[0, :, cols].astype(F32)
    for member in range(1, count):
        total = total + parts_ref[member, :, cols].astype(F32)
    return total / count


def image_kernel(parts_ref, image_ref, copies_ref):
    for chunk in range(parts_ref.shape[2] // PAIR):
        cols = columns(chunk)
        image = mean_of(parts_ref, cols)
        image_ref[:, cols] = image
        for copy in range(copies_ref.shape[0]):
            copies_ref[copy, :, cols] = image


def gradient_kernel(parts_ref, image_ref, both_ref):
    both_ref[0] = image_ref[...]
    halves = parts_ref.shape[2] // PAIR
    for index in range(halves):
        gradient = mean_of(parts_ref, columns(index))
        both_ref[1, :, columns(index)] = gradient[:HALO]
        both_ref[1, :, columns(index + halves)] = gradient[HALO:]


def scaled_rows(adjoint, coef):
    return jnp.concatenate([adjoint[:HALO] * coef, adjoint[HALO:] * coef], axis=0).astype(BF16)


def weighted(masked, state):
    return jnp.concatenate([masked * state[:HALO], masked * state[HALO:]], axis=0)


def adjoint_kernel(level, params, images, state, adjoint, scaled):
    for chunk in range(images.shape[2] // PAIR):
        cols = columns(chunk)
        masked = visible(params, level, cols, images[level, :, cols])
        value = weighted(masked, state[:, cols])
        adjoint[:, cols] = value
        scaled[:, cols] = scaled_rows(value, coef_of(params, level, cols))


def middle_back_kernel(band_ref, weights_ref, rows_ref, lateral_ref):
    pairs = band_ref.shape[1]
    height = rows_ref.shape[0]
    for pair in range(pairs):
        cols = columns(pair)
        rows = rows_ref[:, cols]
        total = dot_t(rows, centre_of(band_ref, pair))
        spread = dot(weights_ref[:, 2 * height : 3 * height], rows)
        total = total + (spread[:height] + spread[height:])
        zero = jnp.zeros((height, BLOCK), F32)
        left, right = (zero, zero)
        if pair > 0:
            before = rows_ref[:, pair * PAIR - BLOCK : pair * PAIR]
            left = dot_t(before, edge_of(band_ref, pair - 1, 1))
        if pair < pairs - 1:
            after = rows_ref[:, (pair + 1) * PAIR : (pair + 1) * PAIR + BLOCK]
            right = dot_t(after, edge_of(band_ref, pair + 1, 0))
        lateral_ref[:, cols] = total + jnp.concatenate([left, right], axis=1)


def back_kernel(level, last, *refs):
    omega, params, weights, lateral, first, second, adjoint, phased = refs[:8]
    if last:
        term = refs[-1].at[0]
        for later, ref in enumerate(refs[8:-1]):
            refs[-1][later + 1] = ref[...]
    else:
        angle, images, state, term, adjoint_next, scaled_next = refs[8:]
    halves = term.shape[1] // PAIR
    for index in range(halves):
        pieces = []
        for chunk in (index, index + halves):
            cols = columns(chunk)
            total = lateral[:, cols] + sides(weights, first, second, cols)
            value = adjoint[:, cols]
            back_re = value[:HALO] + total[HALO:]
            back_im = value[HALO:] - total[:HALO]
            phase_re = phased[2 * HALO : 3 * HALO, cols]
            phase_im = phased[3 * HALO : 4 * HALO, cols]
            pieces.append(omega[0] * (back_im * phase_re - back_re * phase_im))
            if not last:
                cosine, sine = (angle[0:HALO, cols], angle[HALO : 2 * HALO, cols])
                upward = jnp.concatenate(
                    [back_re * cosine + back_im * sine, back_im * cosine - back_re * sine],
                    axis=0,
                )
                upward = upward.astype(BF16).astype(F32)
                masked = visible(params, level - 1, cols, images[level - 1, :, cols])
                following = weighted(masked, state[:, cols]) + upward
                adjoint_next[:, cols] = following
                scaled_next[:, cols] = scaled_rows(following, coef_of(params, level - 1, cols))
        term[:, columns(index)] = jnp.concatenate(pieces, axis=0).astype(BF16)


def call(kernel, name, outs, cost, *args, reuse=None):
    placed = []
    for arg in args:
        scalar = arg.shape == (1,)
        placed.append(arg if scalar else pltpu.with_memory_space_constraint(arg, pltpu.VMEM))
    return pl.pallas_call(
        kernel,
        name=name,
        out_shape=[pltpu.VMEM(shape, kind) for shape, kind in outs],
        in_specs=[SMEM if arg.shape == (1,) else VMEM for arg in args],
        out_specs=[VMEM] * len(outs),
        input_output_aliases=reuse or {},
        cost_estimate=pl.CostEstimate(flops=cost, bytes_accessed=1 << 20, transcendentals=0),
        compiler_params=pltpu.CompilerParams(vmem_limit_bytes=8 << 20),
    )(*placed)


def deliver_kernel(both_ref, image_ref, gradient_ref):
    image_ref[0] = both_ref[0]
    gradient_ref[0] = both_ref[1]


def delivered(both):
    out = jax.ShapeDtypeStruct((1,) + both.shape[1:], both.dtype)
    return pl.pallas_call(
        deliver_kernel,
        name="deliver",
        out_shape=(out, out),
        in_specs=[VMEM],
        out_specs=(VMEM, VMEM),
        compiler_params=pltpu.CompilerParams(vmem_limit_bytes=8 << 20),
    )(pltpu.with_memory_space_constraint(both, pltpu.VMEM))


def frequency_of(depth, lat, sections, size):
    upper = lat >= size // 2
    return (depth + upper * (sections // 2)) % sections


def home_of(row, size):
    half = size // 2
    return (row + 2) % half if row < half else row


def moved(value, inward=True):
    size = lax.axis_size("lat")
    route = [(row, home_of(row, size)) for row in range(size)]
    return lax.ppermute(value, "lat", route if inward else [(b, a) for a, b in route])


def swapped(rows):
    sections, size = (lax.axis_size("depth"), lax.axis_size("lat"))
    place = {}
    for row in range(size):
        lat = home_of(row, size)
        for depth in range(sections):
            place[frequency_of(depth, lat, sections, size), row] = depth * size + lat
    received = []
    for offset in (1, 0):
        route = []
        for member in range(sections):
            for row in range(offset, size - 1, 2):
                one, other = (place[member, row], place[member, row + 1])
                route += [(one, other), (other, one)]
        received.append(lax.ppermute(rows, ("depth", "lat"), route))
    return received


def exchanged(parts):
    return lax.all_to_all(parts, "depth", 0, 0)


def per_device(source_field, receiver_field, freq_index, slowness, ffd_coef, band, image_mask):
    sections = lax.axis_size("depth")
    lat, size = (lax.axis_index("lat"), lax.axis_size("lat"))
    member = frequency_of(lax.axis_index("depth"), lat, sections, size)
    height, width = slowness.shape[1:]
    levels = sections
    omega = 0.1 * (lax.dynamic_slice_in_dim(freq_index, member, 1).astype(F32) + 1.0)
    odd = lax.rem(lat, 2)
    weights_fore = jnp.where(odd == 1, *weights_of(4)[::-1])
    weights_back = jnp.where(odd == 1, *weights_of(2)[::-1])
    fields = []
    for field in (source_field, receiver_field):
        own = lax.dynamic_index_in_dim(field, member, 0, keepdims=False)
        fields.append(own.reshape(2 * height, width))

    wide, half, single = ((4 * height, width), (2 * height, width), (height, width))
    signed = jnp.where(image_mask[0] > 0, ffd_coef[0], -ffd_coef[0])
    own = moved(jnp.stack([slowness[0], signed]))
    fields = [moved(field) for field in fields]
    half_index = odd.astype(jnp.int32).reshape(1)
    share = BLOCK // 2
    pieces = pl.pallas_call(
        share_kernel,
        name="share",
        out_shape=jax.ShapeDtypeStruct((sections,) + band.shape[:2] + (share, BLOCK), BF16),
        in_specs=[SMEM, pl.BlockSpec(memory_space=pl.ANY)],
        out_specs=pl.BlockSpec(memory_space=pl.ANY),
        scratch_shapes=[pltpu.SemaphoreType.DMA((sections,))],
        compiler_params=pltpu.CompilerParams(vmem_limit_bytes=8 << 20),
    )(half_index, pltpu.with_memory_space_constraint(band, pltpu.VMEM))
    pieces = exchanged(pieces)
    params = pl.pallas_call(
        copies_kernel,
        name="copies",
        out_shape=jax.ShapeDtypeStruct((sections,) + own.shape, F32),
        in_specs=[VMEM],
        out_specs=pl.BlockSpec(memory_space=pl.ANY),
        scratch_shapes=[pltpu.SemaphoreType.DMA((sections,))],
        compiler_params=pltpu.CompilerParams(vmem_limit_bytes=8 << 20),
    )(pltpu.with_memory_space_constraint(own, pltpu.VMEM))
    pieces, _ = lax.optimization_barrier((pieces, params))
    params = exchanged(params)
    route = [(lat, lat + 1 - lat % 2 * 2) for lat in range(size)]
    other = lax.ppermute(pieces, "lat", route)
    (band,) = call(
        merge_kernel, "merge", [((2,) + pieces.shape, BF16)], 1000, half_index, pieces, other
    )
    rows, phased = call(
        first_kernel, "first", [(wide, BF16), (wide, F32)], 1000, omega, params, *fields
    )
    stack = (sections, height, width)
    folded = (sections, 2 * height, width // 2)
    states, phases, angles = ([], [phased], [None])
    products = []
    for level in range(levels):
        last = level == levels - 1
        first, second = swapped(rows)
        outs = [(wide, F32)] + ([] if last else [(half, F32)])
        lateral, *more = call(
            functools.partial(middle_kernel, level),
            "middle",
            outs,
            1 << 28,
            omega,
            params,
            band,
            weights_fore,
            rows,
        )
        angles += more
        outs = [(half, F32), (stack, F32)]
        outs += [] if last else [(wide, BF16), (wide, F32)]
        args = [params, weights_fore, lateral, first, second, phased] + more + products
        state, products, *more = call(
            functools.partial(step_kernel, level, last),
            "step",
            outs,
            1 << 20,
            *args,
            reuse={len(args) - 1: 1} if products else None,
        )
        products = [products]
        states.append(state)
        if not last:
            rows, phased = more
            phases.append(phased)

    image, images = call(
        image_kernel, "image", [(single, F32), (stack, F32)], 1000, exchanged(products[0])
    )
    images = exchanged(images)

    level = levels - 1
    adjoint, scaled = call(
        functools.partial(adjoint_kernel, level),
        "adjoint",
        [(half, F32), (half, BF16)],
        1000,
        params,
        images,
        states[level],
    )
    terms = []
    for level in reversed(range(levels)):
        last = level == 0
        first, second = swapped(scaled)
        (lateral,) = call(
            middle_back_kernel, "middle_back", [(half, F32)], 1 << 28, band, weights_back, scaled
        )
        args = [omega, params, weights_back, lateral, first, second, adjoint, phases[level]]
        if last:
            args += terms
            outs = [(folded, BF16)]
        else:
            args += [angles[level], images, states[level - 1]]
            outs = [(folded[1:], BF16), (half, F32), (half, BF16)]
        term, *more = call(
            functools.partial(back_kernel, level, last),
            "back",
            outs,
            1 << 20,
            *args,
        )
        terms = [term] + terms
        if not last:
            adjoint, scaled = more
    (both,) = call(
        gradient_kernel, "gradient", [((2,) + single, F32)], 1000, exchanged(terms[0]), image
    )
    return delivered(moved(both, False))


def solution(mesh):
    return jax.shard_map(
        per_device,
        mesh=mesh,
        in_specs=(
            P(None, None, "lat", None),
            P(None, None, "lat", None),
            P(),
            P("depth", "lat", None),
            P("depth", "lat", None),
            P("depth", None, None, None),
            P("depth", "lat", None),
        ),
        out_specs=(P("depth", "lat", None), P("depth", "lat", None)),
        check_vma=False,
    )
```
